256 devices in a mesh: pts: 8 (over x, core), rows: 32 (over z, y).
Axes of the slice: x: 4, y: 4, z: 8, core: 2. Of those that a mesh axis runs over, the one named last changes fastest.
Arguments:
- solutions: bfloat16 [16, 262144, 128], P('pts', 'rows'), may hold values from -6 to 6
- probe: bfloat16 [64, 262144], P(None, 'rows'), may hold values from -0.01171875 to 0.01171875
- left_factor: float32 [256, 256], replicated, may hold values from -0.375 to 0.375
- singular: float32 [256], replicated, may hold values from 1 to 13.8, as said below
- right_factor: float32 [256, 256], replicated, may hold values from -0.375 to 0.375
- reduced_adjoint: float32 [256, 256], replicated, may hold values from -6 to 6
Outputs:
- solution_adjoint: bfloat16 [16, 262144, 128], P('pts', 'rows')
The draws below stay inside these ranges and needn't reach their ends.
Inputs may be any that keep to these rules, and one draw needn't show every extreme that they name: `singular`: rising, each value at least 0.03 above the one before.
All inputs are finite; a program needn't handle non-finite values.
Results may differ from the reference program's by a relative error of at most 0.0049.
Values sent between devices are 32-bit elements; how exact they have to be, the bound alone decides.
A program may use at most 64 MiB of HBM per device.

```python
import math
import jax
import jax.numpy as jnp
from jax import lax

L = 64
K = 4
HANK = 256
PTS = 16
N = 262144


def draw_singular(key, part):
    jitter = jax.random.uniform(key, (HANK,), jnp.float32)
    return 1.0 + 0.05 * jnp.arange(HANK, dtype=jnp.float32) + 0.02 * jitter


def shard_levels(key, extent, shards, least, top_value):
    def one(position, shards_of):
        draws = jax.random.uniform(jax.random.fold_in(jax.random.fold_in(key, 6), position), (shards_of,), jnp.float32, least / len(shards), top_value / len(shards))
        return jnp.repeat(jnp.exp(draws), extent[position] // shards_of).reshape((-1,) + (1,) * (len(extent) - position - 1))

    loudness = one(*shards[0])
    for cut in shards[1:]:
        loudness = loudness * one(*cut)
    return loudness


def bell_draw(key, extent, scale, most, split=(), kind=jnp.bfloat16):
    entries = jax.random.normal(key, extent, jnp.float32) * scale
    if len(split) > 0:
        entries = shard_levels(key, extent, split, -0.22, 0.18) * entries
    return jnp.clip(entries, min=-most, max=most).astype(kind)


def setup_inputs(seed: int = 0) -> dict:
    key_of = jax.random.split(jax.random.key(seed), 7)
    return {
        "solutions": bell_draw(key_of[0], (PTS, N, 2 * L), 1.0, 6.0, ((0, 8), (1, 32))),
        "probe": bell_draw(key_of[1], (L, N), N ** -0.5, 0.01171875, ((1, 32),)),
        "left_factor": bell_draw(key_of[2], (HANK, HANK), HANK ** -0.5, 0.375, (), jnp.float32),
        "singular": draw_singular(jax.random.fold_in(key_of[6], 71), 0),
        "right_factor": bell_draw(key_of[4], (HANK, HANK), HANK ** -0.5, 0.375, (), jnp.float32),
        "reduced_adjoint": bell_draw(key_of[5], (HANK, HANK), 1.0, 6.0, (), jnp.float32),
    }


def coefficients(first, count, total, orders):
    theta = math.pi * (first + jnp.arange(count, dtype=jnp.float32) + 0.5) / total
    angle = theta[:, None] * orders[None, :]
    return jnp.cos(angle) / total, jnp.sin(angle) / total


def matmul(first, second):
    return jnp.dot(first, second, precision=lax.Precision.HIGHEST, preferred_element_type=jnp.float32)


def svd_back(hankel, left, sing, right, adjoint):
    quot = matmul(left.T, hankel)
    prod_right = matmul(hankel, right)
    zmat = matmul(quot, right)
    zbar = adjoint / sing[None, :]
    sbar = -jnp.sum(adjoint * zmat, axis=0) / (sing * sing)
    ubar = matmul(prod_right, zbar.T)
    wbar = matmul(quot.T, zbar)
    left_term = matmul(left.T, ubar)
    right_term = matmul(right.T, wbar)
    square = sing * sing
    eye_mask = jnp.eye(sing.shape[0], dtype=bool)
    recip = jnp.where(eye_mask, 0.0, 1.0 / jnp.where(eye_mask, 1.0, square[None, :] - square[:, None]))
    core = (recip * (left_term - left_term.T)) * sing[None, :] + jnp.diag(sbar) + sing[:, None] * (recip * (right_term - right_term.T))
    return core, zbar


def build_hankel(moments):
    return jnp.concatenate([jnp.concatenate([moments[i + j] for j in range(K)], axis=1) for i in range(K)], axis=0)


def reference(solutions, probe, left_factor, singular, right_factor, reduced_adjoint):
    hi = lax.Precision.HIGHEST
    gram = lax.map(lambda sol: jnp.dot(probe, sol, preferred_element_type=jnp.float32), solutions)
    orders = jnp.arange(1, 2 * K + 1, dtype=jnp.float32)
    cos_t, sin_t = coefficients(0.0, PTS, PTS, orders)
    moments = jnp.einsum("pk,plc->klc", cos_t[:, 1:], gram[:, :, :L], precision=hi) - jnp.einsum("pk,plc->klc", sin_t[:, 1:], gram[:, :, L:], precision=hi)
    hankel = build_hankel(moments)
    core, zbar = svd_back(hankel, left_factor, singular, right_factor, reduced_adjoint)
    first_bar = matmul(matmul(left_factor, core), right_factor.T)
    second_bar = matmul(matmul(left_factor, zbar), right_factor.T)
    blocks = [jnp.zeros((L, L), jnp.float32) for k in range(2 * K)]
    for i in range(K):
        for j in range(K):
            blocks[i + j] = blocks[i + j] + first_bar[i * L:(i + 1) * L, j * L:(j + 1) * L]
            blocks[i + j + 1] = blocks[i + j + 1] + second_bar[i * L:(i + 1) * L, j * L:(j + 1) * L]
    moment_adjoint = jnp.stack(blocks)
    weights = jnp.concatenate([jnp.einsum("pk,klc->plc", cos_t, moment_adjoint, precision=hi), -jnp.einsum("pk,klc->plc", sin_t, moment_adjoint, precision=hi)], axis=2).astype(jnp.bfloat16)
    return lax.map(lambda wgt: jnp.dot(probe.T, wgt, preferred_element_type=jnp.float32).astype(jnp.bfloat16), weights)
```

```python
import functools
import math

import jax
import jax.numpy as jnp
import numpy as np
from jax import lax
from jax.experimental import pallas as pl
from jax.experimental.pallas import tpu as pltpu
from jax.sharding import PartitionSpec as P

L = 64
K = 4
HANK = 256
PTS = 16
MESH = pl.DeviceIdType.MESH
X, Y, Z, CORES = 4, 4, 8, 2
PIECE = 8
GROUP = X * Y * CORES
CHUNKS = 8


def coefficient_table():
    theta = math.pi * (np.arange(PTS) + 0.5) / PTS
    cos = lambda m: np.cos(m * theta)[:, None] * np.ones((1, L)) / PTS
    sin = lambda m: np.sin(m * theta)[:, None] * np.ones((1, L)) / PTS
    table = np.zeros((PTS, 16, 2 * L))
    for q in range(4):
        table[:, q, :L] = cos(2 * q + 2)
        table[:, 4 + q, :L] = -sin(2 * q + 2)
        if q < 3:
            table[:, q, L:] = -sin(2 * q + 3)
            table[:, 4 + q, L:] = cos(2 * q + 3)
    for k in range(2 * K):
        table[:, 8 + k, :L] = cos(k + 1)
        table[:, 8 + k, L:] = -sin(k + 1)
    return table.astype(np.float32)


def split(value):
    high = value.astype(jnp.bfloat16)
    low = (value - high.astype(jnp.float32)).astype(jnp.bfloat16)
    return high, low


def lhs3(value):
    high, low = split(value)
    return jnp.concatenate([high, high, low], axis=1)


def rhs3(value):
    high, low = split(value)
    return jnp.concatenate([high, low, high], axis=0)


def dot(first, second):
    return jnp.dot(first, second, preferred_element_type=jnp.float32)


def diagonal_sums(full):
    tile = lambda i, h: full[L * i : L * (i + 1), 2 * L * h : 2 * L * (h + 1)]
    return [
        tile(0, 0),
        tile(1, 0),
        tile(2, 0) + tile(0, 1),
        tile(3, 0) + tile(1, 1),
        tile(2, 1),
        tile(3, 1),
    ]


def reduce_kernel(
    sol, probe, left, sing, right, adj, table, w_out,
    solv, probev, leftv, rightv, adjv, singv, tabv,
    send_a, recv_a, recv_b, recv_c,
    lhs_ut, rhs_w, rhs_zt, lhs_zt, lhs_u, rhs_wt, f_row, f_col, second,
    chunk_sem, small_sem, send_sem, recv_sem,
):
    pts = lax.axis_index("pts")
    rows = lax.axis_index("rows")
    x, core = pts // CORES, pts % CORES
    z, y = rows // Y, rows % Y
    me = y * (X * CORES) + pts
    depth = sol.shape[1]
    size = depth // CHUNKS

    plane = []
    for dx, dy in sorted(
        [(i, j) for i in range(X) for j in range(Y)],
        key=lambda d: -(min(d[0], X - d[0]) + min(d[1], Y - d[1])),
    ):
        for dc in range(CORES):
            if dx or dy or dc:
                other = ((x + dx) % X) * CORES + (core + dc) % CORES
                other_y = (y + dy) % Y
                plane.append((other, z * Y + other_y, other_y * (X * CORES) + other))
    line = []
    for dz in sorted(range(1, Z), key=lambda d: -min(d, Z - d)):
        line.append((pts, ((z + dz) % Z) * Y + y))

    copies = []
    for c in range(CHUNKS):
        part = pl.ds(c * size, size)
        group = [pltpu.make_async_copy(probe.at[:, part], probev.at[:, part], chunk_sem.at[c, 0])]
        for p in range(2):
            group.append(
                pltpu.make_async_copy(
                    sol.at[p, part, :], solv.at[part, pl.ds(128 * p, 128)], chunk_sem.at[c, 1 + p]
                )
            )
        for copy in group:
            copy.start()
        copies.append(group)
    small = [
        pltpu.make_async_copy(table.at[pl.ds(pts * 2, 2)], tabv, small_sem.at[0]),
        pltpu.make_async_copy(sing, singv, small_sem.at[1]),
        pltpu.make_async_copy(left, leftv, small_sem.at[2]),
        pltpu.make_async_copy(right, rightv, small_sem.at[3]),
        pltpu.make_async_copy(adj, adjv, small_sem.at[4]),
    ]
    for copy in small:
        copy.start()

    barrier = pltpu.get_barrier_semaphore()
    for p, r in line + [(p, r) for p, r, _ in plane]:
        pl.semaphore_signal(barrier, inc=1, device_id=(p, r), device_id_type=MESH)

    gram = jnp.zeros((L, 256), jnp.float32)
    for c in range(CHUNKS):
        for copy in copies[c]:
            copy.wait()
        part = pl.ds(c * size, size)
        gram = gram + dot(probev[:, part], solv[part, :])
    small[0].wait()
    for q in range(4):
        total = None
        for p in range(2):
            own = gram[:, 128 * p : 128 * (p + 1)]
            term = own * tabv[p, q : q + 1, :] + pltpu.roll(own, L, 1) * tabv[p, 4 + q : 5 + q, :]
            total = term if total is None else total + term
        send_a[L * q : L * (q + 1), :] = total

    pl.semaphore_wait(barrier, len(plane) + len(line))
    mine = pl.ds(pl.multiple_of(me * PIECE, PIECE), PIECE)
    for p, r, there in plane:
        pltpu.make_async_remote_copy(
            src_ref=send_a.at[pl.ds(pl.multiple_of(there * PIECE, PIECE), PIECE)],
            dst_ref=recv_a.at[mine],
            send_sem=send_sem.at[0],
            recv_sem=recv_sem.at[0],
            device_id=(p, r),
            device_id_type=MESH,
        ).start()
    recv_a[mine, :] = send_a[mine, :]

    for copy in small[1:]:
        copy.wait()
    s_row = jnp.broadcast_to(singv[...], (HANK, HANK))
    s_col = s_row.T
    zbar = adjv[...] / s_row
    u = leftv[...]
    w = rightv[...]
    lhs_ut[...] = lhs3(u.T)
    rhs_w[...] = rhs3(w)
    lhs_u[...] = lhs3(u)

    many = pl.ds(0, (GROUP - 1) * PIECE)
    everything = lambda ref, n, i: pltpu.make_async_copy(
        ref.at[pl.ds(0, n * PIECE)], ref.at[pl.ds(0, n * PIECE)], i
    )
    everything(recv_a, GROUP - 1, recv_sem.at[0]).wait()
    here = pl.ds(pl.multiple_of(z * PIECE, PIECE), PIECE)
    recv_b[here, :] = jnp.sum(recv_a[...].reshape(GROUP, PIECE, 128), axis=0)
    for p, r in line:
        pltpu.make_async_remote_copy(
            src_ref=recv_b.at[here],
            dst_ref=recv_b.at[here],
            send_sem=send_sem.at[1],
            recv_sem=recv_sem.at[1],
            device_id=(p, r),
            device_id_type=MESH,
        ).start()

    zt = zbar.T
    lhs_zt[...] = lhs3(zt)
    rhs_zt[...] = rhs3(zt)
    rhs_wt[...] = rhs3(w.T)

    everything(recv_b, Z - 1, recv_sem.at[1]).wait()
    recv_c[mine, :] = jnp.sum(recv_b[...].reshape(Z, PIECE, 128), axis=0)
    for p, r, _ in plane:
        pltpu.make_async_remote_copy(
            src_ref=recv_c.at[mine],
            dst_ref=recv_c.at[mine],
            send_sem=send_sem.at[2],
            recv_sem=recv_sem.at[2],
            device_id=(p, r),
            device_id_type=MESH,
        ).start()

    row_id = lax.broadcasted_iota(jnp.int32, (HANK, HANK), 0)
    col_id = lax.broadcasted_iota(jnp.int32, (HANK, HANK), 1)
    eye = row_id == col_id
    recip = jnp.where(eye, 0.0, 1.0 / jnp.where(eye, 1.0, s_row * s_row - s_col * s_col))
    f_row[...] = recip * s_row
    f_col[...] = recip * s_col
    second_bar = dot(lhs3(dot(lhs_u[...], rhs3(zbar))), rhs_wt[...])
    for m, value in enumerate(diagonal_sums(second_bar)):
        second[m] = value

    everything(recv_c, GROUP - 1, recv_sem.at[2]).wait()
    lane = lax.broadcasted_iota(jnp.int32, (L, 2 * L), 1)
    low = lane < L
    even = [recv_c[L * q : L * (q + 1), :] for q in range(4)]
    turned = [pltpu.roll(value, L, 1) for value in even]
    pairs = []
    for q in range(3):
        pairs.append(even[q])
        pairs.append(jnp.where(low, turned[q], turned[q + 1]))
    hankel = jnp.concatenate(
        [jnp.concatenate([pairs[i], pairs[i + 2]], axis=1) for i in range(K)], axis=0
    )
    quot = dot(lhs_ut[...], rhs3(hankel))
    zmat = dot(lhs3(quot), rhs_w[...])
    sing_row = singv[...]
    sbar = -jnp.sum(adjv[...] * zmat, axis=0, keepdims=True) / (sing_row * sing_row)
    left_term = dot(lhs3(zmat), rhs_zt[...])
    right_term = dot(lhs_zt[...], rhs3(zmat))
    core_mat = (
        f_row[...] * (left_term - left_term.T)
        - f_col[...] * (right_term - right_term.T)
        + jnp.where(eye, jnp.broadcast_to(sbar, (HANK, HANK)), 0.0)
    )
    first_bar = dot(lhs3(dot(lhs_u[...], rhs3(core_mat))), rhs_wt[...])

    sums = diagonal_sums(first_bar)
    sums = [sums[0]] + [sums[m] + second[m - 1] for m in range(1, 6)] + [second[5]]
    weights = [jnp.zeros((L, 2 * L), jnp.float32) for p in range(2)]
    zero = jnp.zeros((L, 2 * L), jnp.float32)
    for k in range(2 * K):
        here_k = sums[k] if k < 7 else zero
        before = sums[k - 1] if k > 0 else zero
        mixed = jnp.where(low, here_k, before)
        both = mixed + pltpu.roll(mixed, L, 1)
        for p in range(2):
            weights[p] = weights[p] + both * tabv[p, 8 + k : 9 + k, :]
    for p in range(2):
        w_out[:, 128 * p : 128 * (p + 1)] = weights[p].astype(jnp.bfloat16)

    everything(recv_a, GROUP - 1, send_sem.at[0]).wait()
    everything(recv_b, Z - 1, send_sem.at[1]).wait()
    everything(recv_c, GROUP - 1, send_sem.at[2]).wait()


def output_kernel(probe_ref, w_ref, out_ref):
    res = lax.dot_general(
        probe_ref[...], w_ref[...], (((0,), (0,)), ((), ())), preferred_element_type=jnp.float32
    )
    for p in range(2):
        out_ref[p] = res[:, 128 * p : 128 * (p + 1)].astype(jnp.bfloat16)


def per_device(solutions, probe, left_factor, singular, right_factor, reduced_adjoint):
    table = jnp.asarray(coefficient_table())
    depth = solutions.shape[1]
    hbm = pl.BlockSpec(memory_space=pl.ANY)
    f32 = lambda *shape: pltpu.VMEM(shape, jnp.float32)
    bf16 = lambda *shape: pltpu.VMEM(shape, jnp.bfloat16)
    weights = pl.pallas_call(
        reduce_kernel,
        name="moments",
        out_shape=jax.ShapeDtypeStruct((L, 256), jnp.bfloat16),
        in_specs=[hbm] * 7,
        out_specs=pl.BlockSpec(memory_space=pltpu.VMEM),
        scratch_shapes=[
            bf16(depth, 256), bf16(L, depth), f32(HANK, HANK), f32(HANK, HANK), f32(HANK, HANK),
            f32(1, HANK), f32(2, 16, 128),
            f32(GROUP * PIECE, 128), f32(GROUP * PIECE, 128), f32(Z * PIECE, 128), f32(GROUP * PIECE, 128),
            bf16(HANK, 3 * HANK), bf16(3 * HANK, HANK), bf16(3 * HANK, HANK), bf16(HANK, 3 * HANK),
            bf16(HANK, 3 * HANK), bf16(3 * HANK, HANK), f32(HANK, HANK), f32(HANK, HANK), f32(6, L, 2 * L),
            pltpu.SemaphoreType.DMA((CHUNKS, 3)), pltpu.SemaphoreType.DMA((5,)),
            pltpu.SemaphoreType.DMA((3,)), pltpu.SemaphoreType.DMA((3,)),
        ],
        compiler_params=pltpu.CompilerParams(collective_id=0, has_side_effects=True),
    )(solutions, probe, left_factor, singular.reshape(1, HANK), right_factor, reduced_adjoint, table)
    tile = 1024
    return pl.pallas_call(
        output_kernel,
        name="output",
        grid=(depth // tile,),
        out_shape=jax.ShapeDtypeStruct((2, depth, 128), jnp.bfloat16),
        in_specs=[
            pl.BlockSpec((L, tile), lambda i: (0, i)),
            pl.BlockSpec((L, 256), lambda i: (0, 0)),
        ],
        out_specs=pl.BlockSpec((2, tile, 128), lambda i: (0, i, 0)),
    )(probe, weights)


def solution(mesh):
    in_specs = (P("pts", "rows", None), P(None, "rows"), P(), P(), P(), P())
    out_specs = P("pts", "rows", None)
    return jax.shard_map(
        per_device, mesh=mesh, in_specs=in_specs, out_specs=out_specs, check_vma=False
    )
```

```python
import functools
import math

import jax
import jax.numpy as jnp
import numpy as np
from jax import lax
from jax.experimental import pallas as pl
from jax.experimental.pallas import tpu as pltpu
from jax.sharding import PartitionSpec as P

L = 64
K = 4
HANK = 256
PTS = 16
MESH = pl.DeviceIdType.MESH
X, Y, Z, CORES = 4, 4, 8, 2
PIECE = 8
GROUP = X * Y * CORES
CHUNKS = 8


def coefficient_table():
    theta = math.pi * (np.arange(PTS) + 0.5) / PTS
    cos = lambda m: np.cos(m * theta)[:, None] * np.ones((1, L)) / PTS
    sin = lambda m: np.sin(m * theta)[:, None] * np.ones((1, L)) / PTS
    table = np.zeros((PTS, 16, 2 * L))
    for q in range(4):
        table[:, q, :L] = cos(2 * q + 2)
        table[:, 4 + q, :L] = -sin(2 * q + 2)
        if q < 3:
            table[:, q, L:] = -sin(2 * q + 3)
            table[:, 4 + q, L:] = cos(2 * q + 3)
    for k in range(2 * K):
        table[:, 8 + k, :L] = cos(k + 1)
        table[:, 8 + k, L:] = -sin(k + 1)
    return table.astype(np.float32)


def split(value):
    high = value.astype(jnp.bfloat16)
    low = (value - high.astype(jnp.float32)).astype(jnp.bfloat16)
    return high, low


def lhs3(value):
    high, low = split(value)
    return jnp.concatenate([high, high, low], axis=1)


def rhs3(value):
    high, low = split(value)
    return jnp.concatenate([high, low, high], axis=0)


def dot(first, second):
    return jnp.dot(first, second, preferred_element_type=jnp.float32)


def diagonal_sums(full):
    tile = lambda i, h: full[L * i : L * (i + 1), 2 * L * h : 2 * L * (h + 1)]
    return [
        tile(0, 0),
        tile(1, 0),
        tile(2, 0) + tile(0, 1),
        tile(3, 0) + tile(1, 1),
        tile(2, 1),
        tile(3, 1),
    ]


def reduce_kernel(
    sol, probe, left, sing, right, adj, table, w_out, turned_out,
    solv, probev, leftv, rightv, adjv, singv, tabv,
    send_a, recv_a, recv_b, recv_c,
    lhs_ut, rhs_w, rhs_zt, lhs_zt, lhs_u, rhs_wt, f_row, f_col, second,
    chunk_sem, small_sem, send_sem, recv_sem,
):
    pts = lax.axis_index("pts")
    rows = lax.axis_index("rows")
    x, core = pts // CORES, pts % CORES
    z, y = rows // Y, rows % Y
    me = y * (X * CORES) + pts
    depth = sol.shape[1]
    size = depth // CHUNKS

    plane = []
    for dx, dy in sorted(
        [(i, j) for i in range(X) for j in range(Y)],
        key=lambda d: -(min(d[0], X - d[0]) + min(d[1], Y - d[1])),
    ):
        for dc in range(CORES):
            if dx or dy or dc:
                other = ((x + dx) % X) * CORES + (core + dc) % CORES
                other_y = (y + dy) % Y
                plane.append((other, z * Y + other_y, other_y * (X * CORES) + other))
    line = []
    for dz in sorted(range(1, Z), key=lambda d: -min(d, Z - d)):
        line.append((pts, ((z + dz) % Z) * Y + y))

    half = depth // 2
    step = half // 8

    def turn(first, last):
        for t in range(first, last):
            pair = [probev[:, h * half + t * step : h * half + (t + 1) * step] for h in range(2)]
            turned_out[t * step : (t + 1) * step, :] = jnp.concatenate(pair, axis=0).T

    copies = []
    for c in range(CHUNKS):
        part = pl.ds(c * size, size)
        group = [pltpu.make_async_copy(probe.at[:, part], probev.at[:, part], chunk_sem.at[c, 0])]
        for p in range(2):
            group.append(
                pltpu.make_async_copy(
                    sol.at[p, part, :], solv.at[part, pl.ds(128 * p, 128)], chunk_sem.at[c, 1 + p]
                )
            )
        for copy in group:
            copy.start()
        copies.append(group)
    small = [
        pltpu.make_async_copy(table.at[pl.ds(pts * 2, 2)], tabv, small_sem.at[0]),
        pltpu.make_async_copy(sing, singv, small_sem.at[1]),
        pltpu.make_async_copy(left, leftv, small_sem.at[2]),
        pltpu.make_async_copy(right, rightv, small_sem.at[3]),
        pltpu.make_async_copy(adj, adjv, small_sem.at[4]),
    ]
    for copy in small:
        copy.start()

    barrier = pltpu.get_barrier_semaphore()
    for p, r in line + [(p, r) for p, r, _ in plane]:
        pl.semaphore_signal(barrier, inc=1, device_id=(p, r), device_id_type=MESH)

    gram = jnp.zeros((L, 256), jnp.float32)
    for c in range(CHUNKS):
        for copy in copies[c]:
            copy.wait()
        part = pl.ds(c * size, size)
        gram = gram + dot(probev[:, part], solv[part, :])
    small[0].wait()
    for q in range(4):
        total = None
        for p in range(2):
            own = gram[:, 128 * p : 128 * (p + 1)]
            term = own * tabv[p, q : q + 1, :] + pltpu.roll(own, L, 1) * tabv[p, 4 + q : 5 + q, :]
            total = term if total is None else total + term
        send_a[L * q : L * (q + 1), :] = total

    pl.semaphore_wait(barrier, len(plane) + len(line))
    mine = pl.ds(pl.multiple_of(me * PIECE, PIECE), PIECE)
    for p, r, there in plane:
        pltpu.make_async_remote_copy(
            src_ref=send_a.at[pl.ds(pl.multiple_of(there * PIECE, PIECE), PIECE)],
            dst_ref=recv_a.at[mine],
            send_sem=send_sem.at[0],
            recv_sem=recv_sem.at[0],
            device_id=(p, r),
            device_id_type=MESH,
        ).start()
    recv_a[mine, :] = send_a[mine, :]

    for copy in small[1:]:
        copy.wait()
    s_row = jnp.broadcast_to(singv[...], (HANK, HANK))
    s_col = s_row.T
    zbar = adjv[...] / s_row
    u = leftv[...]
    w = rightv[...]
    lhs_ut[...] = lhs3(u.T)
    rhs_w[...] = rhs3(w)
    lhs_u[...] = lhs3(u)
    turn(0, 3)

    many = pl.ds(0, (GROUP - 1) * PIECE)
    everything = lambda ref, n, i: pltpu.make_async_copy(
        ref.at[pl.ds(0, n * PIECE)], ref.at[pl.ds(0, n * PIECE)], i
    )
    everything(recv_a, GROUP - 1, recv_sem.at[0]).wait()
    here = pl.ds(pl.multiple_of(z * PIECE, PIECE), PIECE)
    recv_b[here, :] = jnp.sum(recv_a[...].reshape(GROUP, PIECE, 128), axis=0)
    for p, r in line:
        pltpu.make_async_remote_copy(
            src_ref=recv_b.at[here],
            dst_ref=recv_b.at[here],
            send_sem=send_sem.at[1],
            recv_sem=recv_sem.at[1],
            device_id=(p, r),
            device_id_type=MESH,
        ).start()

    zt = zbar.T
    lhs_zt[...] = lhs3(zt)
    rhs_zt[...] = rhs3(zt)
    rhs_wt[...] = rhs3(w.T)
    turn(3, 5)

    everything(recv_b, Z - 1, recv_sem.at[1]).wait()
    recv_c[mine, :] = jnp.sum(recv_b[...].reshape(Z, PIECE, 128), axis=0)
    for p, r, _ in plane:
        pltpu.make_async_remote_copy(
            src_ref=recv_c.at[mine],
            dst_ref=recv_c.at[mine],
            send_sem=send_sem.at[2],
            recv_sem=recv_sem.at[2],
            device_id=(p, r),
            device_id_type=MESH,
        ).start()

    row_id = lax.broadcasted_iota(jnp.int32, (HANK, HANK), 0)
    col_id = lax.broadcasted_iota(jnp.int32, (HANK, HANK), 1)
    eye = row_id == col_id
    recip = jnp.where(eye, 0.0, 1.0 / jnp.where(eye, 1.0, s_row * s_row - s_col * s_col))
    f_row[...] = recip * s_row
    f_col[...] = recip * s_col
    second_bar = dot(lhs3(dot(lhs_u[...], rhs3(zbar))), rhs_wt[...])
    for m, value in enumerate(diagonal_sums(second_bar)):
        second[m] = value
    turn(5, 8)

    everything(recv_c, GROUP - 1, recv_sem.at[2]).wait()
    lane = lax.broadcasted_iota(jnp.int32, (L, 2 * L), 1)
    low = lane < L
    even = [recv_c[L * q : L * (q + 1), :] for q in range(4)]
    turned = [pltpu.roll(value, L, 1) for value in even]
    pairs = []
    for q in range(3):
        pairs.append(even[q])
        pairs.append(jnp.where(low, turned[q], turned[q + 1]))
    hankel = jnp.concatenate(
        [jnp.concatenate([pairs[i], pairs[i + 2]], axis=1) for i in range(K)], axis=0
    )
    quot = dot(lhs_ut[...], rhs3(hankel))
    zmat = dot(lhs3(quot), rhs_w[...])
    sing_row = singv[...]
    sbar = -jnp.sum(adjv[...] * zmat, axis=0, keepdims=True) / (sing_row * sing_row)
    left_term = dot(lhs3(zmat), rhs_zt[...])
    right_term = dot(lhs_zt[...], rhs3(zmat))
    core_mat = (
        f_row[...] * (left_term - left_term.T)
        - f_col[...] * (right_term - right_term.T)
        + jnp.where(eye, jnp.broadcast_to(sbar, (HANK, HANK)), 0.0)
    )
    first_bar = dot(lhs3(dot(lhs_u[...], rhs3(core_mat))), rhs_wt[...])

    sums = diagonal_sums(first_bar)
    sums = [sums[0]] + [sums[m] + second[m - 1] for m in range(1, 6)] + [second[5]]
    weights = [jnp.zeros((L, 2 * L), jnp.float32) for p in range(2)]
    zero = jnp.zeros((L, 2 * L), jnp.float32)
    for k in range(2 * K):
        here_k = sums[k] if k < 7 else zero
        before = sums[k - 1] if k > 0 else zero
        mixed = jnp.where(low, here_k, before)
        both = mixed + pltpu.roll(mixed, L, 1)
        for p in range(2):
            weights[p] = weights[p] + both * tabv[p, 8 + k : 9 + k, :]
    for p in range(2):
        w_out[:, 128 * p : 128 * (p + 1)] = weights[p].astype(jnp.bfloat16)

    everything(recv_a, GROUP - 1, send_sem.at[0]).wait()
    everything(recv_b, Z - 1, send_sem.at[1]).wait()
    everything(recv_c, GROUP - 1, send_sem.at[2]).wait()


def output_kernel(turned, w_ref, out, held, sem):
    half = turned.shape[0]
    size = half // CHUNKS
    zero = jnp.zeros((L, 256), jnp.bfloat16)
    wide = [jnp.concatenate([w_ref[...], zero], axis=0), jnp.concatenate([zero, w_ref[...]], axis=0)]
    copies = []
    for c in range(CHUNKS):
        block = turned[c * size : (c + 1) * size, :]
        for h in range(2):
            res = dot(block, wide[h]).astype(jnp.bfloat16)
            part = pl.ds(h * half + c * size, size)
            for p in range(2):
                held[p, part, :] = res[:, 128 * p : 128 * (p + 1)]
                copy = pltpu.make_async_copy(held.at[p, part, :], out.at[p, part, :], sem.at[c, h, p])
                copy.start()
                copies.append(copy)
    for copy in copies:
        copy.wait()


def per_device(solutions, probe, left_factor, singular, right_factor, reduced_adjoint):
    table = jnp.asarray(coefficient_table())
    depth = solutions.shape[1]
    hbm = pl.BlockSpec(memory_space=pltpu.HBM)
    vmem = pl.BlockSpec(memory_space=pltpu.VMEM)
    f32 = lambda *shape: pltpu.VMEM(shape, jnp.float32)
    bf16 = lambda *shape: pltpu.VMEM(shape, jnp.bfloat16)
    weights, turned = pl.pallas_call(
        reduce_kernel,
        name="moments",
        out_shape=[
            jax.ShapeDtypeStruct((L, 256), jnp.bfloat16),
            jax.ShapeDtypeStruct((depth // 2, 128), jnp.bfloat16),
        ],
        in_specs=[hbm] * 7,
        out_specs=[vmem] * 2,
        scratch_shapes=[
            bf16(depth, 256), bf16(L, depth), f32(HANK, HANK), f32(HANK, HANK), f32(HANK, HANK),
            f32(1, HANK), f32(2, 16, 128),
            f32(GROUP * PIECE, 128), f32(GROUP * PIECE, 128), f32(Z * PIECE, 128), f32(GROUP * PIECE, 128),
            bf16(HANK, 3 * HANK), bf16(3 * HANK, HANK), bf16(3 * HANK, HANK), bf16(HANK, 3 * HANK),
            bf16(HANK, 3 * HANK), bf16(3 * HANK, HANK), f32(HANK, HANK), f32(HANK, HANK), f32(6, L, 2 * L),
            pltpu.SemaphoreType.DMA((CHUNKS, 3)), pltpu.SemaphoreType.DMA((5,)),
            pltpu.SemaphoreType.DMA((3,)), pltpu.SemaphoreType.DMA((3,)),
        ],
        compiler_params=pltpu.CompilerParams(
            collective_id=0, has_side_effects=True, vmem_limit_bytes=24 << 20
        ),
    )(
        *(
            pltpu.with_memory_space_constraint(array, pltpu.HBM)
            for array in (
                solutions, probe, left_factor, singular.reshape(1, HANK), right_factor, reduced_adjoint, table
            )
        )
    )
    return pl.pallas_call(
        output_kernel,
        name="output",
        out_shape=jax.ShapeDtypeStruct((2, depth, 128), jnp.bfloat16),
        in_specs=[vmem] * 2,
        out_specs=pl.BlockSpec(memory_space=pltpu.HBM),
        scratch_shapes=[bf16(2, depth, 128), pltpu.SemaphoreType.DMA((CHUNKS, 2, 2))],
        compiler_params=pltpu.CompilerParams(vmem_limit_bytes=24 << 20),
    )(turned, weights)


def solution(mesh):
    in_specs = (P("pts", "rows", None), P(None, "rows"), P(), P(), P(), P())
    out_specs = P("pts", "rows", None)
    return jax.shard_map(
        per_device, mesh=mesh, in_specs=in_specs, out_specs=out_specs, check_vma=False
    )
```

```python
import functools
import math

import jax
import jax.numpy as jnp
import numpy as np
from jax import lax
from jax.experimental import pallas as pl
from jax.experimental.pallas import tpu as pltpu
from jax.sharding import PartitionSpec as P

L = 64
K = 4
HANK = 256
PTS = 16
MESH = pl.DeviceIdType.MESH
X, Y, Z, CORES = 4, 4, 8, 2
PIECE = 8
GROUP = X * Y * CORES
CHUNKS = 8
OUT_ROWS = 128


def coefficient_table():
    theta = math.pi * (np.arange(PTS) + 0.5) / PTS
    cos = lambda m: np.cos(m * theta)[:, None] * np.ones((1, L)) / PTS
    sin = lambda m: np.sin(m * theta)[:, None] * np.ones((1, L)) / PTS
    table = np.zeros((PTS, 16, 2 * L))
    for q in range(4):
        table[:, q, :L] = cos(2 * q + 2)
        table[:, 4 + q, :L] = -sin(2 * q + 2)
        if q < 3:
            table[:, q, L:] = -sin(2 * q + 3)
            table[:, 4 + q, L:] = cos(2 * q + 3)
    for k in range(2 * K):
        table[:, 8 + k, :L] = cos(k + 1)
        table[:, 8 + k, L:] = -sin(k + 1)
    return table.astype(np.float32)


def split(value):
    high = value.astype(jnp.bfloat16)
    low = (value - high.astype(jnp.float32)).astype(jnp.bfloat16)
    return high, low


def dot(first, second):
    return jnp.dot(first, second, preferred_element_type=jnp.float32)


def product(accs, first, second):
    quarter = HANK // 4
    for unit in range(2):
        pltpu.matmul_push_rhs(second[0], 0, unit)
        pltpu.matmul_push_rhs(second[1], 1, unit)
    for unit in range(2):
        for b in range(2):
            part = slice((2 * unit + b) * quarter, (2 * unit + b + 1) * quarter)
            pltpu.matmul_acc_lhs(accs[2 * unit + b], first[0][part], 0 if b == 0 else None)
            pltpu.matmul_acc_lhs(accs[2 * unit + b], first[1][part])
    for unit in range(2):
        for b in range(2):
            part = slice((2 * unit + b) * quarter, (2 * unit + b + 1) * quarter)
            pltpu.matmul_acc_lhs(accs[2 * unit + b], first[0][part], 1 if b == 0 else None)
    return jnp.concatenate([pltpu.matmul_pop(acc) for acc in accs], axis=0)


def diagonal_sums(full):
    tile = lambda i, h: full[L * i : L * (i + 1), 2 * L * h : 2 * L * (h + 1)]
    return [
        tile(0, 0),
        tile(1, 0),
        tile(2, 0) + tile(0, 1),
        tile(3, 0) + tile(1, 1),
        tile(2, 1),
        tile(3, 1),
    ]


def reduce_body(
    sol, probe, left, sing, right, adj, table, w_out, turned_out,
    solv, probev, factors, singv, tabv, send_a, recv_a, recv_b, recv_c,
    ut_ref, w_ref, zt_ref, u_ref, wt_ref, f_row, f_col, second,
    chunk_sem, small_sem, send_sem, recv_sem, *accs
):
    pts = lax.axis_index("pts")
    rows = lax.axis_index("rows")
    x, core = lax.div(pts, CORES), lax.rem(pts, CORES)
    z, y = lax.div(rows, Y), lax.rem(rows, Y)
    me = y * (X * CORES) + pts
    depth = sol.shape[1]
    size = depth // CHUNKS
    half = depth // 2

    copies = []
    for c in range(CHUNKS):
        if c % (CHUNKS // 2) == 0:
            part = pl.ds((2 * c // CHUNKS) * half, half)
            copy = pltpu.make_async_copy(probe.at[:, part], probev.at[:, part], chunk_sem.at[CHUNKS + 2 * c // CHUNKS])
            copy.start()
            copies.append(copy)
        part = pl.ds(c * size, size)
        copy = pltpu.make_async_copy(sol.at[:, part], solv.at[:, part], chunk_sem.at[c])
        copy.start()
        copies.append(copy)
    tab = pltpu.make_async_copy(table.at[pl.ds(pts * 2, 2)], tabv, small_sem.at[0])
    tab.start()

    xs = [lax.rem(x + d, X) * CORES for d in range(X)]
    cores = [core, 1 - core]
    ys = [lax.rem(y + d, Y) for d in range(Y)]
    zs = [lax.rem(z + d, Z) * Y + y for d in range(Z)]
    plane = []
    for dx, dy in sorted(
        [(i, j) for i in range(X) for j in range(Y)],
        key=lambda d: -(min(d[0], X - d[0]) + min(d[1], Y - d[1])),
    ):
        for dc in range(CORES):
            if dx or dy or dc:
                other = xs[dx] + cores[dc]
                plane.append((other, z * Y + ys[dy], ys[dy] * (X * CORES) + other))
    line = [(pts, zs[d]) for d in sorted(range(1, Z), key=lambda d: -min(d, Z - d))]

    barrier = pltpu.get_barrier_semaphore()
    for p, r in line[:1] + [(p, r) for p, r, _ in plane] + line[1:]:
        pl.semaphore_signal(barrier, inc=1, device_id=(p, r), device_id_type=MESH)
    small = [pltpu.make_async_copy(sing, singv, small_sem.at[1])]
    small += [pltpu.make_async_copy(ref, factors.at[i], small_sem.at[2]) for i, ref in enumerate((left, right, adj))]
    for copy in small:
        copy.start()

    tile = 0
    done = iter(copies)
    for c in range(CHUNKS):
        if c % (CHUNKS // 2) == 0:
            next(done).wait()
        next(done).wait()
        for start in range(c * size, (c + 1) * size, HANK):
            part = pl.ds(start, HANK)
            unit, register = tile % 2, tile // 2 % 2
            pltpu.matmul_push_rhs(jnp.concatenate([solv[0, part, :], solv[1, part, :]], axis=1), register, unit)
            pltpu.matmul_acc_lhs(accs[2 * unit], probev[:, part], register)
            tile += 1
    gram = pltpu.matmul_pop(accs[0]) + pltpu.matmul_pop(accs[2])
    tab.wait()
    for q in range(4):
        total = None
        for p in range(2):
            own = gram[:, 128 * p : 128 * (p + 1)]
            term = own * tabv[p, q : q + 1, :] + pltpu.roll(own, L, 1) * tabv[p, 4 + q : 5 + q, :]
            total = term if total is None else total + term
        send_a[L * q : L * (q + 1), :] = total

    def piece(index):
        return pl.ds(pl.multiple_of(index * PIECE, PIECE), PIECE)

    def send(peers, source, target, phase):
        @pl.when(rows >= 0)
        def _():
            for peer in peers:
                pltpu.make_async_remote_copy(
                    src_ref=source(peer),
                    dst_ref=target,
                    send_sem=send_sem.at[0],
                    recv_sem=recv_sem.at[phase],
                    device_id=peer[:2],
                    device_id_type=MESH,
                ).start()

    def arrived(ref, count, phase):
        ref = ref.at[pl.ds(0, count * PIECE)]
        pltpu.make_async_copy(ref, ref, recv_sem.at[phase]).wait()

    mine, here = piece(me), piece(z)
    pl.semaphore_wait(barrier, len(plane) + len(line))
    send(plane, lambda peer: send_a.at[piece(peer[2])], recv_a.at[mine], 0)

    def keep(ref, value):
        ref[0], ref[1] = split(value)

    def turn(first, last):
        step = half // 8
        for t in range(first, last):
            pair = [probev[:, h * half + t * step : h * half + (t + 1) * step] for h in range(2)]
            turned_out[t * step : (t + 1) * step, :] = jnp.concatenate(pair, axis=0).T

    recv_a[mine, :] = send_a[mine, :]
    small[0].wait()
    pltpu.make_async_copy(factors, factors, small_sem.at[2]).wait()
    s_row = jnp.broadcast_to(singv[...], (HANK, HANK))
    zbar = factors[2] / s_row
    keep(ut_ref, factors[0].T)
    keep(u_ref, factors[0])
    keep(w_ref, factors[1])
    keep(wt_ref, factors[1].T)
    keep(zt_ref, zbar.T)
    turn(0, 4)

    arrived(recv_a, GROUP - 1, 0)
    recv_b[here, :] = jnp.sum(recv_a[...].reshape(GROUP, PIECE, 128), axis=0)
    send(line, lambda peer: recv_b.at[here], recv_b.at[here], 1)

    row_id = lax.broadcasted_iota(jnp.int32, (HANK, HANK), 0)
    col_id = lax.broadcasted_iota(jnp.int32, (HANK, HANK), 1)
    eye = row_id == col_id
    s_col = s_row.T
    recip = jnp.where(eye, 0.0, 1.0 / jnp.where(eye, 1.0, s_row * s_row - s_col * s_col))
    f_row[...] = recip * s_row
    f_col[...] = recip * s_col
    second_bar = product(accs, split(product(accs, u_ref, split(zbar))), wt_ref)
    for m, value in enumerate(diagonal_sums(second_bar)):
        second[m] = value

    arrived(recv_b, Z - 1, 1)
    recv_c[mine, :] = jnp.sum(recv_b[...].reshape(Z, PIECE, 128), axis=0)
    send(plane, lambda peer: recv_c.at[mine], recv_c.at[mine], 2)

    turn(4, 8)

    arrived(recv_c, GROUP - 1, 2)
    lane = lax.broadcasted_iota(jnp.int32, (L, 2 * L), 1)
    low = lane < L
    even = [recv_c[L * q : L * (q + 1), :] for q in range(4)]
    turned = [pltpu.roll(value, L, 1) for value in even]
    pairs = []
    for q in range(3):
        pairs.append(even[q])
        pairs.append(jnp.where(low, turned[q], turned[q + 1]))
    hankel = jnp.concatenate(
        [jnp.concatenate([pairs[i], pairs[i + 2]], axis=1) for i in range(K)], axis=0
    )
    quot = product(accs, ut_ref, split(hankel))
    zmat = product(accs, split(quot), w_ref)
    parts = split(zmat)
    left_term = product(accs, parts, zt_ref)
    right_term = product(accs, zt_ref, parts)
    sing_row = singv[...]
    sbar = -jnp.sum(factors[2] * zmat, axis=0, keepdims=True) / (sing_row * sing_row)
    core_mat = (
        f_row[...] * (left_term - left_term.T)
        - f_col[...] * (right_term - right_term.T)
        + jnp.where(eye, jnp.broadcast_to(sbar, (HANK, HANK)), 0.0)
    )
    first_bar = product(accs, split(product(accs, u_ref, split(core_mat))), wt_ref)

    sums = diagonal_sums(first_bar)
    sums = [sums[0]] + [sums[m] + second[m - 1] for m in range(1, 6)] + [second[5]]
    weights = [jnp.zeros((L, 2 * L), jnp.float32) for p in range(2)]
    zero = jnp.zeros((L, 2 * L), jnp.float32)
    for k in range(2 * K):
        here_k = sums[k] if k < 7 else zero
        before = sums[k - 1] if k > 0 else zero
        mixed = jnp.where(low, here_k, before)
        both = mixed + pltpu.roll(mixed, L, 1)
        for p in range(2):
            weights[p] = weights[p] + both * tabv[p, 8 + k : 9 + k, :]
    for p in range(2):
        w_out[:, 128 * p : 128 * (p + 1)] = weights[p].astype(jnp.bfloat16)

    sent = solv.at[0, pl.ds(0, 2 * PIECE * (2 * len(plane) + len(line)))]
    pltpu.make_async_copy(sent, sent, send_sem.at[0]).wait()


def reduce_kernel(*refs):
    quarters = [pltpu.ACC(unit)((HANK // 4, HANK), jnp.float32) for unit in (0, 0, 1, 1)]
    pl.run_scoped(functools.partial(reduce_body, *refs), *quarters)


def output_kernel(turned, w_ref, out, held, sem):
    half = turned.shape[0]
    size = OUT_ROWS
    zero = jnp.zeros((L, 256), jnp.bfloat16)
    wide = [jnp.concatenate([w_ref[...], zero], axis=0), jnp.concatenate([zero, w_ref[...]], axis=0)]
    for c in range(half // size):
        block = turned[c * size : (c + 1) * size, :]
        for h in range(2):
            res = dot(block, wide[h]).astype(jnp.bfloat16)
            part = pl.ds(h * half + c * size, size)
            for p in range(2):
                held[p, part, :] = res[:, 128 * p : 128 * (p + 1)]
            pltpu.make_async_copy(held.at[:, part], out.at[:, part], sem.at[0]).start()
    pltpu.make_async_copy(held, out, sem.at[0]).wait()


def per_device(solutions, probe, left_factor, singular, right_factor, reduced_adjoint):
    table = jnp.asarray(coefficient_table())
    depth = solutions.shape[1]
    hbm = pl.BlockSpec(memory_space=pltpu.HBM)
    vmem = pl.BlockSpec(memory_space=pltpu.VMEM)
    f32 = lambda *shape: pltpu.VMEM(shape, jnp.float32)
    bf16 = lambda *shape: pltpu.VMEM(shape, jnp.bfloat16)
    weights, turned = pl.pallas_call(
        reduce_kernel,
        name="moments",
        out_shape=[
            jax.ShapeDtypeStruct((L, 256), jnp.bfloat16),
            jax.ShapeDtypeStruct((depth // 2, 128), jnp.bfloat16),
        ],
        in_specs=[hbm] * 7,
        out_specs=[vmem] * 2,
        scratch_shapes=[
            bf16(2, depth, 128), bf16(L, depth), f32(3, HANK, HANK), f32(1, HANK), f32(2, 16, 128),
            f32(GROUP * PIECE, 128), f32(GROUP * PIECE, 128), f32(Z * PIECE, 128), f32(GROUP * PIECE, 128),
            *[bf16(2, HANK, HANK)] * 5, f32(HANK, HANK), f32(HANK, HANK), f32(6, L, 2 * L),
            pltpu.SemaphoreType.DMA((CHUNKS + 2,)), pltpu.SemaphoreType.DMA((3,)),
            pltpu.SemaphoreType.DMA((1,)), pltpu.SemaphoreType.DMA((3,)),
        ],
        compiler_params=pltpu.CompilerParams(
            collective_id=0, has_side_effects=True, vmem_limit_bytes=24 << 20
        ),
    )(
        *(
            pltpu.with_memory_space_constraint(array, pltpu.HBM)
            for array in (
                solutions, probe, left_factor, singular.reshape(1, HANK), right_factor, reduced_adjoint, table
            )
        )
    )
    return pl.pallas_call(
        output_kernel,
        name="output",
        out_shape=jax.ShapeDtypeStruct((2, depth, 128), jnp.bfloat16),
        in_specs=[vmem] * 2,
        out_specs=pl.BlockSpec(memory_space=pltpu.HBM),
        scratch_shapes=[bf16(2, depth, 128), pltpu.SemaphoreType.DMA((1,))],
        compiler_params=pltpu.CompilerParams(vmem_limit_bytes=24 << 20),
    )(turned, weights)


def solution(mesh):
    in_specs = (P("pts", "rows", None), P(None, "rows"), P(), P(), P(), P())
    out_specs = P("pts", "rows", None)
    return jax.shard_map(
        per_device, mesh=mesh, in_specs=in_specs, out_specs=out_specs, check_vma=False
    )
```

```python
import functools
import math

import jax
import jax.numpy as jnp
import numpy as np
from jax import lax
from jax.experimental import pallas as pl
from jax.experimental.pallas import tpu as pltpu
from jax.sharding import PartitionSpec as P

L = 64
K = 4
HANK = 256
PTS = 16
MESH = pl.DeviceIdType.MESH
X, Y, Z, CORES = 4, 4, 8, 2
OWNERS = 16
PIECE = 16
GROUP = X * Y * CORES
CHUNKS = 8
OUT_ROWS = 128


def coefficient_table():
    theta = math.pi * (np.arange(PTS) + 0.5) / PTS
    cos = lambda m: np.cos(m * theta)[:, None] * np.ones((1, L)) / PTS
    sin = lambda m: np.sin(m * theta)[:, None] * np.ones((1, L)) / PTS
    table = np.zeros((PTS, 16, 2 * L))
    for q in range(4):
        table[:, q, :L] = cos(2 * q + 2)
        table[:, 4 + q, :L] = -sin(2 * q + 2)
        if q < 3:
            table[:, q, L:] = -sin(2 * q + 3)
            table[:, 4 + q, L:] = cos(2 * q + 3)
    for k in range(2 * K):
        table[:, 8 + k, :L] = cos(k + 1)
        table[:, 8 + k, L:] = -sin(k + 1)
    return table.astype(np.float32)


def split(value):
    high = value.astype(jnp.bfloat16)
    low = (value - high.astype(jnp.float32)).astype(jnp.bfloat16)
    return high, low


def dot(first, second):
    return jnp.dot(first, second, preferred_element_type=jnp.float32)


def product(accs, first, second):
    quarter = HANK // 4
    for unit in range(2):
        pltpu.matmul_push_rhs(second[0], 0, unit)
        pltpu.matmul_push_rhs(second[1], 1, unit)
    for unit in range(2):
        for b in range(2):
            part = slice((2 * unit + b) * quarter, (2 * unit + b + 1) * quarter)
            pltpu.matmul_acc_lhs(accs[2 * unit + b], first[0][part], 0 if b == 0 else None)
            pltpu.matmul_acc_lhs(accs[2 * unit + b], first[1][part])
    for unit in range(2):
        for b in range(2):
            part = slice((2 * unit + b) * quarter, (2 * unit + b + 1) * quarter)
            pltpu.matmul_acc_lhs(accs[2 * unit + b], first[0][part], 1 if b == 0 else None)
    return jnp.concatenate([pltpu.matmul_pop(acc) for acc in accs], axis=0)


def diagonal_sums(full):
    tile = lambda i, h: full[L * i : L * (i + 1), 2 * L * h : 2 * L * (h + 1)]
    return [
        tile(0, 0),
        tile(1, 0),
        tile(2, 0) + tile(0, 1),
        tile(3, 0) + tile(1, 1),
        tile(2, 1),
        tile(3, 1),
    ]


def reduce_body(
    sol, probe, left, sing, right, adj, table, w_out, turned_out,
    solv, probev, factors, singv, tabv, send_a, recv_a, recv_b, recv_c,
    ut_ref, w_ref, zt_ref, u_ref, wt_ref, f_row, f_col, second,
    chunk_sem, small_sem, send_sem, recv_sem, *accs
):
    pts = lax.axis_index("pts")
    rows = lax.axis_index("rows")
    x, core = lax.div(pts, CORES), lax.rem(pts, CORES)
    z, y = lax.div(rows, Y), lax.rem(rows, Y)
    me = y * (X * CORES) + pts
    depth = sol.shape[1]
    size = depth // CHUNKS
    half = depth // 2

    copies = []
    for c in range(CHUNKS):
        if c % (CHUNKS // 2) == 0:
            part = pl.ds((2 * c // CHUNKS) * half, half)
            copy = pltpu.make_async_copy(probe.at[:, part], probev.at[:, part], chunk_sem.at[CHUNKS + 2 * c // CHUNKS])
            copy.start()
            copies.append(copy)
        part = pl.ds(c * size, size)
        copy = pltpu.make_async_copy(sol.at[:, part], solv.at[:, part], chunk_sem.at[c])
        copy.start()
        copies.append(copy)
    tab = pltpu.make_async_copy(table.at[pl.ds(pts * 2, 2)], tabv, small_sem.at[0])
    tab.start()

    owner = y < 2
    spots = sorted(
        [(p, j) for p in range(X * CORES) for j in range(Y)],
        key=lambda d: (min(d[0] // CORES, X - d[0] // CORES) + min(d[1], Y - d[1]), -(d[0] % CORES)),
    )
    plane = [(p, z * Y + j, j * (X * CORES) + p) for p, j in spots]
    owners = [peer + (j * X * CORES + p,) for peer, (p, j) in zip(plane, spots) if j < 2]
    line = [(pts, lax.rem(z + d, Z) * Y + y, -1) for d in sorted(range(1, Z), key=lambda d: -min(d, Z - d))]
    index = me

    def each(peers, action):
        for peer in peers:
            pl.when(me != peer[2])(functools.partial(action, peer))

    barrier = pltpu.get_barrier_semaphore()

    def announce(peer):
        pl.semaphore_signal(barrier, inc=1, device_id=peer[:2], device_id_type=MESH)

    @pl.when(owner)
    def _():
        each(plane[::-1], announce)
        for peer in line:
            announce(peer)

    small = [pltpu.make_async_copy(sing, singv, small_sem.at[1])]
    small += [pltpu.make_async_copy(ref, factors.at[i], small_sem.at[2]) for i, ref in enumerate((left, right, adj))]
    for copy in small:
        copy.start()

    tile = 0
    done = iter(copies)
    for c in range(CHUNKS):
        if c % (CHUNKS // 2) == 0:
            next(done).wait()
        next(done).wait()
        for start in range(c * size, (c + 1) * size, HANK):
            part = pl.ds(start, HANK)
            unit, register = tile % 2, tile // 2 % 2
            pltpu.matmul_push_rhs(jnp.concatenate([solv[0, part, :], solv[1, part, :]], axis=1), register, unit)
            pltpu.matmul_acc_lhs(accs[2 * unit], probev[:, part], register)
            tile += 1
    gram = pltpu.matmul_pop(accs[0]) + pltpu.matmul_pop(accs[2])
    tab.wait()
    for q in range(4):
        total = None
        for p in range(2):
            own = gram[:, 128 * p : 128 * (p + 1)]
            term = own * tabv[p, q : q + 1, :] + pltpu.roll(own, L, 1) * tabv[p, 4 + q : 5 + q, :]
            total = term if total is None else total + term
        send_a[L * q : L * (q + 1), :] = total

    def piece(index):
        return pl.ds(pl.multiple_of(index * PIECE, PIECE), PIECE)

    def send(source, target, phase, peer):
        pltpu.make_async_remote_copy(
            src_ref=source(peer),
            dst_ref=target,
            send_sem=send_sem.at[0],
            recv_sem=recv_sem.at[phase],
            device_id=peer[:2],
            device_id_type=MESH,
        ).start()

    def arrived(ref, count, phase):
        ref = ref.at[pl.ds(0, count * PIECE)]
        pltpu.make_async_copy(ref, ref, recv_sem.at[phase]).wait()

    mine, here = piece(index), piece(z)

    @pl.when(owner)
    def _():
        pl.semaphore_wait(barrier, OWNERS - 1 + Z - 1)

    @pl.when(jnp.logical_not(owner))
    def _():
        pl.semaphore_wait(barrier, OWNERS)

    each(owners, functools.partial(send, lambda peer: send_a.at[piece(peer[3])], recv_a.at[piece(me)], 0))

    def keep(ref, value):
        ref[0], ref[1] = split(value)

    def turn(first, last):
        step = half // 8
        for t in range(first, last):
            pair = [probev[:, h * half + t * step : h * half + (t + 1) * step] for h in range(2)]
            turned_out[t * step : (t + 1) * step, :] = jnp.concatenate(pair, axis=0).T

    @pl.when(owner)
    def _():
        recv_a[piece(me), :] = send_a[mine, :]

    small[0].wait()
    pltpu.make_async_copy(factors, factors, small_sem.at[2]).wait()
    s_row = jnp.broadcast_to(singv[...], (HANK, HANK))
    zbar = factors[2] / s_row
    keep(ut_ref, factors[0].T)
    keep(u_ref, factors[0])
    keep(w_ref, factors[1])
    keep(wt_ref, factors[1].T)
    keep(zt_ref, zbar.T)
    turn(0, 4)

    @pl.when(owner)
    def _():
        arrived(recv_a, GROUP - 1, 0)
        recv_b[here, :] = jnp.sum(recv_a[...].reshape(GROUP, PIECE, 128), axis=0)
        for peer in line:
            send(lambda peer: recv_b.at[here], recv_b.at[here], 1, peer)

    row_id = lax.broadcasted_iota(jnp.int32, (HANK, HANK), 0)
    col_id = lax.broadcasted_iota(jnp.int32, (HANK, HANK), 1)
    eye = row_id == col_id
    s_col = s_row.T
    recip = jnp.where(eye, 0.0, 1.0 / jnp.where(eye, 1.0, s_row * s_row - s_col * s_col))
    f_row[...] = recip * s_row
    f_col[...] = recip * s_col
    second_bar = product(accs, split(product(accs, u_ref, split(zbar))), wt_ref)
    for m, value in enumerate(diagonal_sums(second_bar)):
        second[m] = value

    @pl.when(owner)
    def _():
        arrived(recv_b, Z - 1, 1)
        recv_c[mine, :] = jnp.sum(recv_b[...].reshape(Z, PIECE, 128), axis=0)
        each(plane, functools.partial(send, lambda peer: recv_c.at[mine], recv_c.at[mine], 2))

    turn(4, 8)

    @pl.when(owner)
    def _():
        arrived(recv_c, OWNERS - 1, 2)

    @pl.when(jnp.logical_not(owner))
    def _():
        arrived(recv_c, OWNERS, 2)

    lane = lax.broadcasted_iota(jnp.int32, (L, 2 * L), 1)
    low = lane < L
    even = [recv_c[L * q : L * (q + 1), :] for q in range(4)]
    turned = [pltpu.roll(value, L, 1) for value in even]
    pairs = []
    for q in range(3):
        pairs.append(even[q])
        pairs.append(jnp.where(low, turned[q], turned[q + 1]))
    hankel = jnp.concatenate(
        [jnp.concatenate([pairs[i], pairs[i + 2]], axis=1) for i in range(K)], axis=0
    )
    quot = product(accs, ut_ref, split(hankel))
    zmat = product(accs, split(quot), w_ref)
    parts = split(zmat)
    left_term = product(accs, parts, zt_ref)
    right_term = product(accs, zt_ref, parts)
    sing_row = singv[...]
    sbar = -jnp.sum(factors[2] * zmat, axis=0, keepdims=True) / (sing_row * sing_row)
    core_mat = (
        f_row[...] * (left_term - left_term.T)
        - f_col[...] * (right_term - right_term.T)
        + jnp.where(eye, jnp.broadcast_to(sbar, (HANK, HANK)), 0.0)
    )
    first_bar = product(accs, split(product(accs, u_ref, split(core_mat))), wt_ref)

    sums = diagonal_sums(first_bar)
    sums = [sums[0]] + [sums[m] + second[m - 1] for m in range(1, 6)] + [second[5]]
    weights = [jnp.zeros((L, 2 * L), jnp.float32) for p in range(2)]
    zero = jnp.zeros((L, 2 * L), jnp.float32)
    for k in range(2 * K):
        here_k = sums[k] if k < 7 else zero
        before = sums[k - 1] if k > 0 else zero
        mixed = jnp.where(low, here_k, before)
        both = mixed + pltpu.roll(mixed, L, 1)
        for p in range(2):
            weights[p] = weights[p] + both * tabv[p, 8 + k : 9 + k, :]
    for p in range(2):
        w_out[:, 128 * p : 128 * (p + 1)] = weights[p].astype(jnp.bfloat16)

    def all_sent(count):
        sent = solv.at[0, pl.ds(0, 2 * PIECE * count)]
        pltpu.make_async_copy(sent, sent, send_sem.at[0]).wait()

    @pl.when(owner)
    def _():
        all_sent(OWNERS - 1 + Z - 1 + GROUP - 1)

    @pl.when(jnp.logical_not(owner))
    def _():
        all_sent(OWNERS)


def reduce_kernel(*refs):
    quarters = [pltpu.ACC(unit)((HANK // 4, HANK), jnp.float32) for unit in (0, 0, 1, 1)]
    pl.run_scoped(functools.partial(reduce_body, *refs), *quarters)


def output_kernel(turned, w_ref, out, held, sem):
    half = turned.shape[0]
    size = OUT_ROWS
    zero = jnp.zeros((L, 256), jnp.bfloat16)
    wide = [jnp.concatenate([w_ref[...], zero], axis=0), jnp.concatenate([zero, w_ref[...]], axis=0)]
    for c in range(half // size):
        block = turned[c * size : (c + 1) * size, :]
        for h in range(2):
            res = dot(block, wide[h]).astype(jnp.bfloat16)
            part = pl.ds(h * half + c * size, size)
            for p in range(2):
                held[p, part, :] = res[:, 128 * p : 128 * (p + 1)]
            pltpu.make_async_copy(held.at[:, part], out.at[:, part], sem.at[0]).start()
    pltpu.make_async_copy(held, out, sem.at[0]).wait()


def per_device(solutions, probe, left_factor, singular, right_factor, reduced_adjoint):
    table = jnp.asarray(coefficient_table())
    depth = solutions.shape[1]
    hbm = pl.BlockSpec(memory_space=pltpu.HBM)
    vmem = pl.BlockSpec(memory_space=pltpu.VMEM)
    f32 = lambda *shape: pltpu.VMEM(shape, jnp.float32)
    bf16 = lambda *shape: pltpu.VMEM(shape, jnp.bfloat16)
    weights, turned = pl.pallas_call(
        reduce_kernel,
        name="moments",
        out_shape=[
            jax.ShapeDtypeStruct((L, 256), jnp.bfloat16),
            jax.ShapeDtypeStruct((depth // 2, 128), jnp.bfloat16),
        ],
        in_specs=[hbm] * 7,
        out_specs=[vmem] * 2,
        scratch_shapes=[
            bf16(2, depth, 128), bf16(L, depth), f32(3, HANK, HANK), f32(1, HANK), f32(2, 16, 128),
            f32(OWNERS * PIECE, 128), f32(GROUP * PIECE, 128), f32(Z * PIECE, 128), f32(OWNERS * PIECE, 128),
            *[bf16(2, HANK, HANK)] * 5, f32(HANK, HANK), f32(HANK, HANK), f32(6, L, 2 * L),
            pltpu.SemaphoreType.DMA((CHUNKS + 2,)), pltpu.SemaphoreType.DMA((3,)),
            pltpu.SemaphoreType.DMA((1,)), pltpu.SemaphoreType.DMA((3,)),
        ],
        compiler_params=pltpu.CompilerParams(
            collective_id=0, has_side_effects=True, vmem_limit_bytes=24 << 20
        ),
    )(
        *(
            pltpu.with_memory_space_constraint(array, pltpu.HBM)
            for array in (
                solutions, probe, left_factor, singular.reshape(1, HANK), right_factor, reduced_adjoint, table
            )
        )
    )
    return pl.pallas_call(
        output_kernel,
        name="output",
        out_shape=jax.ShapeDtypeStruct((2, depth, 128), jnp.bfloat16),
        in_specs=[vmem] * 2,
        out_specs=pl.BlockSpec(memory_space=pltpu.HBM),
        scratch_shapes=[bf16(2, depth, 128), pltpu.SemaphoreType.DMA((1,))],
        compiler_params=pltpu.CompilerParams(vmem_limit_bytes=24 << 20),
    )(turned, weights)


def solution(mesh):
    in_specs = (P("pts", "rows", None), P(None, "rows"), P(), P(), P(), P())
    out_specs = P("pts", "rows", None)
    return jax.shard_map(
        per_device, mesh=mesh, in_specs=in_specs, out_specs=out_specs, check_vma=False
    )
```

```python
import functools
import math

import jax
import jax.numpy as jnp
import numpy as np
from jax import lax
from jax.experimental import pallas as pl
from jax.experimental.pallas import tpu as pltpu
from jax.sharding import PartitionSpec as P

L = 64
K = 4
HANK = 256
PTS = 16
MESH = pl.DeviceIdType.MESH
X, Y, Z, CORES = 4, 4, 8, 2
OWNERS = 14
PIECE = 16
GROUP = X * Y * CORES
CHUNKS = 8
OUT_ROWS = 128


def coefficient_table():
    theta = math.pi * (np.arange(PTS) + 0.5) / PTS
    cos = lambda m: np.cos(m * theta)[:, None] * np.ones((1, L)) / PTS
    sin = lambda m: np.sin(m * theta)[:, None] * np.ones((1, L)) / PTS
    table = np.zeros((PTS, 16, 2 * L))
    for q in range(4):
        table[:, q, :L] = cos(2 * q + 2)
        table[:, 4 + q, :L] = -sin(2 * q + 2)
        if q < 3:
            table[:, q, L:] = -sin(2 * q + 3)
            table[:, 4 + q, L:] = cos(2 * q + 3)
    for k in range(2 * K):
        table[:, 8 + k, :L] = cos(k + 1)
        table[:, 8 + k, L:] = -sin(k + 1)
    return table.astype(np.float32)


def split(value):
    high = value.astype(jnp.bfloat16)
    low = (value - high.astype(jnp.float32)).astype(jnp.bfloat16)
    return high, low


def dot(first, second):
    return jnp.dot(first, second, preferred_element_type=jnp.float32)


def product(accs, first, second):
    quarter = HANK // 4
    for unit in range(2):
        pltpu.matmul_push_rhs(second[0], 0, unit)
        pltpu.matmul_push_rhs(second[1], 1, unit)
    for unit in range(2):
        for b in range(2):
            part = slice((2 * unit + b) * quarter, (2 * unit + b + 1) * quarter)
            pltpu.matmul_acc_lhs(accs[2 * unit + b], first[0][part], 0 if b == 0 else None)
            pltpu.matmul_acc_lhs(accs[2 * unit + b], first[1][part])
    for unit in range(2):
        for b in range(2):
            part = slice((2 * unit + b) * quarter, (2 * unit + b + 1) * quarter)
            pltpu.matmul_acc_lhs(accs[2 * unit + b], first[0][part], 1 if b == 0 else None)
    return jnp.concatenate([pltpu.matmul_pop(acc) for acc in accs], axis=0)


def diagonal_sums(full):
    tile = lambda i, h: full[L * i : L * (i + 1), 2 * L * h : 2 * L * (h + 1)]
    return [
        tile(0, 0),
        tile(1, 0),
        tile(2, 0) + tile(0, 1),
        tile(3, 0) + tile(1, 1),
        tile(2, 1),
        tile(3, 1),
    ]


def reduce_body(
    sol, probe, left, sing, right, adj, table, w_out, turned_out,
    solv, probev, factors, singv, tabv, send_a, recv_a, recv_b, recv_c,
    ut_ref, w_ref, zt_ref, u_ref, wt_ref, f_row, f_col, second,
    chunk_sem, small_sem, send_sem, recv_sem, *accs
):
    pts = lax.axis_index("pts")
    rows = lax.axis_index("rows")
    x, core = lax.div(pts, CORES), lax.rem(pts, CORES)
    z, y = lax.div(rows, Y), lax.rem(rows, Y)
    me = y * (X * CORES) + pts
    depth = sol.shape[1]
    size = depth // CHUNKS
    half = depth // 2

    copies = []
    for c in range(CHUNKS):
        if c % (CHUNKS // 2) == 0:
            part = pl.ds((2 * c // CHUNKS) * half, half)
            copy = pltpu.make_async_copy(probe.at[:, part], probev.at[:, part], chunk_sem.at[CHUNKS + 2 * c // CHUNKS])
            copy.start()
            copies.append(copy)
        part = pl.ds(c * size, size)
        copy = pltpu.make_async_copy(sol.at[:, part], solv.at[:, part], chunk_sem.at[c])
        copy.start()
        copies.append(copy)
    tab = pltpu.make_async_copy(table.at[pl.ds(pts * 2, 2)], tabv, small_sem.at[0])
    tab.start()

    owner = (y == 0) | ((y == 1) & (x != 2))
    spots = sorted(
        [(p, j) for p in range(X * CORES) for j in range(Y)],
        key=lambda d: (min(d[0] // CORES, X - d[0] // CORES) + min(d[1], Y - d[1]), -(d[0] % CORES)),
    )
    plane = [(p, z * Y + j, j * (X * CORES) + p) for p, j in spots]
    owners = [
        peer + (j * (X * CORES - p // (3 * CORES) * CORES) + p,)
        for peer, (p, j) in zip(plane, spots)
        if j == 0 or (j == 1 and p // CORES != 2)
    ]
    line = [(pts, lax.rem(z + d, Z) * Y + y, -1) for d in sorted(range(1, Z), key=lambda d: -min(d, Z - d))]
    index = y * (X * CORES - lax.div(x, 3) * CORES) + pts

    def each(peers, action):
        for peer in peers:
            pl.when(me != peer[2])(functools.partial(action, peer))

    barrier = pltpu.get_barrier_semaphore()

    def announce(peer):
        pl.semaphore_signal(barrier, inc=1, device_id=peer[:2], device_id_type=MESH)

    @pl.when(owner)
    def _():
        each(plane[::-1], announce)
        for peer in line:
            announce(peer)

    small = [pltpu.make_async_copy(sing, singv, small_sem.at[1])]
    small += [pltpu.make_async_copy(ref, factors.at[i], small_sem.at[2]) for i, ref in enumerate((left, right, adj))]
    for copy in small:
        copy.start()

    tile = 0
    done = iter(copies)
    for c in range(CHUNKS):
        if c % (CHUNKS // 2) == 0:
            next(done).wait()
        next(done).wait()
        for start in range(c * size, (c + 1) * size, HANK):
            part = pl.ds(start, HANK)
            unit, register = tile % 2, tile // 2 % 2
            pltpu.matmul_push_rhs(jnp.concatenate([solv[0, part, :], solv[1, part, :]], axis=1), register, unit)
            pltpu.matmul_acc_lhs(accs[2 * unit], probev[:, part], register)
            tile += 1
    gram = pltpu.matmul_pop(accs[0]) + pltpu.matmul_pop(accs[2])
    tab.wait()
    for q in range(4):
        total = None
        for p in range(2):
            own = gram[:, 128 * p : 128 * (p + 1)]
            term = own * tabv[p, q : q + 1, :] + pltpu.roll(own, L, 1) * tabv[p, 4 + q : 5 + q, :]
            total = term if total is None else total + term
        if q < 3:
            send_a[L * q : L * (q + 1), :] = total
        else:
            send_a[L * q :, :] = total[: L // 2] + pltpu.roll(total[L // 2 :], L, 1)

    def piece(index):
        return pl.ds(pl.multiple_of(index * PIECE, PIECE), PIECE)

    def send(source, target, phase, peer):
        pltpu.make_async_remote_copy(
            src_ref=source(peer),
            dst_ref=target,
            send_sem=send_sem.at[0],
            recv_sem=recv_sem.at[phase],
            device_id=peer[:2],
            device_id_type=MESH,
        ).start()

    def arrived(ref, count, phase):
        ref = ref.at[pl.ds(0, count * PIECE)]
        pltpu.make_async_copy(ref, ref, recv_sem.at[phase]).wait()

    mine, here = piece(index), piece(z)

    @pl.when(owner)
    def _():
        pl.semaphore_wait(barrier, OWNERS - 1 + Z - 1)

    @pl.when(jnp.logical_not(owner))
    def _():
        pl.semaphore_wait(barrier, OWNERS)

    each(owners[::-1], functools.partial(send, lambda peer: send_a.at[piece(peer[3])], recv_a.at[piece(me)], 0))

    def keep(ref, value):
        ref[0], ref[1] = split(value)

    def turn(first, last):
        step = half // 8
        for t in range(first, last):
            pair = [probev[:, h * half + t * step : h * half + (t + 1) * step] for h in range(2)]
            turned_out[t * step : (t + 1) * step, :] = jnp.concatenate(pair, axis=0).T

    @pl.when(owner)
    def _():
        recv_a[piece(me), :] = send_a[mine, :]

    small[0].wait()
    pltpu.make_async_copy(factors, factors, small_sem.at[2]).wait()
    s_row = jnp.broadcast_to(singv[...], (HANK, HANK))
    zbar = factors[2] / s_row
    keep(ut_ref, factors[0].T)
    keep(u_ref, factors[0])
    keep(w_ref, factors[1])
    keep(wt_ref, factors[1].T)
    keep(zt_ref, zbar.T)
    turn(0, 4)

    @pl.when(owner)
    def _():
        arrived(recv_a, GROUP - 1, 0)
        recv_b[here, :] = jnp.sum(recv_a[...].reshape(GROUP, PIECE, 128), axis=0)
        for peer in line:
            send(lambda peer: recv_b.at[here], recv_b.at[here], 1, peer)

    row_id = lax.broadcasted_iota(jnp.int32, (HANK, HANK), 0)
    col_id = lax.broadcasted_iota(jnp.int32, (HANK, HANK), 1)
    eye = row_id == col_id
    s_col = s_row.T
    recip = jnp.where(eye, 0.0, 1.0 / jnp.where(eye, 1.0, s_row * s_row - s_col * s_col))
    f_row[...] = recip * s_row
    f_col[...] = recip * s_col
    second_bar = product(accs, split(product(accs, u_ref, split(zbar))), wt_ref)
    for m, value in enumerate(diagonal_sums(second_bar)):
        second[m] = value

    @pl.when(owner)
    def _():
        arrived(recv_b, Z - 1, 1)
        recv_c[mine, :] = jnp.sum(recv_b[...].reshape(Z, PIECE, 128), axis=0)
        each(plane, functools.partial(send, lambda peer: recv_c.at[mine], recv_c.at[mine], 2))

    turn(4, 8)

    @pl.when(owner)
    def _():
        arrived(recv_c, OWNERS - 1, 2)

    @pl.when(jnp.logical_not(owner))
    def _():
        arrived(recv_c, OWNERS, 2)

    lane = lax.broadcasted_iota(jnp.int32, (L, 2 * L), 1)
    low = lane < L
    even = [recv_c[L * q : L * (q + 1), :] for q in range(3)]
    last = recv_c[3 * L :, :]
    turned = [pltpu.roll(value, L, 1) for value in even]
    turned.append(jnp.concatenate([pltpu.roll(last, L, 1), last], axis=0))
    pairs = []
    for q in range(3):
        pairs.append(even[q])
        pairs.append(jnp.where(low, turned[q], turned[q + 1]))
    hankel = jnp.concatenate(
        [jnp.concatenate([pairs[i], pairs[i + 2]], axis=1) for i in range(K)], axis=0
    )
    quot = product(accs, ut_ref, split(hankel))
    zmat = product(accs, split(quot), w_ref)
    parts = split(zmat)
    left_term = product(accs, parts, zt_ref)
    right_term = product(accs, zt_ref, parts)
    sing_row = singv[...]
    sbar = -jnp.sum(factors[2] * zmat, axis=0, keepdims=True) / (sing_row * sing_row)
    core_mat = (
        f_row[...] * (left_term - left_term.T)
        - f_col[...] * (right_term - right_term.T)
        + jnp.where(eye, jnp.broadcast_to(sbar, (HANK, HANK)), 0.0)
    )
    first_bar = product(accs, split(product(accs, u_ref, split(core_mat))), wt_ref)

    sums = diagonal_sums(first_bar)
    sums = [sums[0]] + [sums[m] + second[m - 1] for m in range(1, 6)] + [second[5]]
    weights = [jnp.zeros((L, 2 * L), jnp.float32) for p in range(2)]
    zero = jnp.zeros((L, 2 * L), jnp.float32)
    for k in range(2 * K):
        here_k = sums[k] if k < 7 else zero
        before = sums[k - 1] if k > 0 else zero
        mixed = jnp.where(low, here_k, before)
        both = mixed + pltpu.roll(mixed, L, 1)
        for p in range(2):
            weights[p] = weights[p] + both * tabv[p, 8 + k : 9 + k, :]
    for p in range(2):
        w_out[:, 128 * p : 128 * (p + 1)] = weights[p].astype(jnp.bfloat16)

    def all_sent(count):
        sent = solv.at[0, pl.ds(0, 2 * PIECE * count)]
        pltpu.make_async_copy(sent, sent, send_sem.at[0]).wait()

    @pl.when(owner)
    def _():
        all_sent(OWNERS - 1 + Z - 1 + GROUP - 1)

    @pl.when(jnp.logical_not(owner))
    def _():
        all_sent(OWNERS)


def reduce_kernel(*refs):
    quarters = [pltpu.ACC(unit)((HANK // 4, HANK), jnp.float32) for unit in (0, 0, 1, 1)]
    pl.run_scoped(functools.partial(reduce_body, *refs), *quarters)


def output_kernel(turned, w_ref, out, held, sem):
    half = turned.shape[0]
    size = OUT_ROWS
    zero = jnp.zeros((L, 256), jnp.bfloat16)
    wide = [jnp.concatenate([w_ref[...], zero], axis=0), jnp.concatenate([zero, w_ref[...]], axis=0)]
    for c in range(half // size):
        block = turned[c * size : (c + 1) * size, :]
        for h in range(2):
            res = dot(block, wide[h]).astype(jnp.bfloat16)
            part = pl.ds(h * half + c * size, size)
            for p in range(2):
                held[p, part, :] = res[:, 128 * p : 128 * (p + 1)]
            pltpu.make_async_copy(held.at[:, part], out.at[:, part], sem.at[0]).start()
    pltpu.make_async_copy(held, out, sem.at[0]).wait()


def per_device(solutions, probe, left_factor, singular, right_factor, reduced_adjoint):
    table = jnp.asarray(coefficient_table())
    depth = solutions.shape[1]
    hbm = pl.BlockSpec(memory_space=pltpu.HBM)
    vmem = pl.BlockSpec(memory_space=pltpu.VMEM)
    f32 = lambda *shape: pltpu.VMEM(shape, jnp.float32)
    bf16 = lambda *shape: pltpu.VMEM(shape, jnp.bfloat16)
    weights, turned = pl.pallas_call(
        reduce_kernel,
        name="moments",
        out_shape=[
            jax.ShapeDtypeStruct((L, 256), jnp.bfloat16),
            jax.ShapeDtypeStruct((depth // 2, 128), jnp.bfloat16),
        ],
        in_specs=[hbm] * 7,
        out_specs=[vmem] * 2,
        scratch_shapes=[
            bf16(2, depth, 128), bf16(L, depth), f32(3, HANK, HANK), f32(1, HANK), f32(2, 16, 128),
            f32(OWNERS * PIECE, 128), f32(GROUP * PIECE, 128), f32(Z * PIECE, 128), f32(OWNERS * PIECE, 128),
            *[bf16(2, HANK, HANK)] * 5, f32(HANK, HANK), f32(HANK, HANK), f32(6, L, 2 * L),
            pltpu.SemaphoreType.DMA((CHUNKS + 2,)), pltpu.SemaphoreType.DMA((3,)),
            pltpu.SemaphoreType.DMA((1,)), pltpu.SemaphoreType.DMA((3,)),
        ],
        compiler_params=pltpu.CompilerParams(
            collective_id=0, has_side_effects=True, vmem_limit_bytes=24 << 20
        ),
    )(
        *(
            pltpu.with_memory_space_constraint(array, pltpu.HBM)
            for array in (
                solutions, probe, left_factor, singular.reshape(1, HANK), right_factor, reduced_adjoint, table
            )
        )
    )
    return pl.pallas_call(
        output_kernel,
        name="output",
        out_shape=jax.ShapeDtypeStruct((2, depth, 128), jnp.bfloat16),
        in_specs=[vmem] * 2,
        out_specs=pl.BlockSpec(memory_space=pltpu.HBM),
        scratch_shapes=[bf16(2, depth, 128), pltpu.SemaphoreType.DMA((1,))],
        compiler_params=pltpu.CompilerParams(vmem_limit_bytes=24 << 20),
    )(turned, weights)


def solution(mesh):
    in_specs = (P("pts", "rows", None), P(None, "rows"), P(), P(), P(), P())
    out_specs = P("pts", "rows", None)
    return jax.shard_map(
        per_device, mesh=mesh, in_specs=in_specs, out_specs=out_specs, check_vma=False
    )
```

```python
import functools
import math

import jax
import jax.numpy as jnp
import numpy as np
from jax import lax
from jax.experimental import pallas as pl
from jax.experimental.pallas import tpu as pltpu
from jax.sharding import PartitionSpec as P

L = 64
K = 4
HANK = 256
PTS = 16
MESH = pl.DeviceIdType.MESH
X, Y, Z, CORES = 4, 4, 8, 2
OWNERS = 14
PIECE = 16
GROUP = X * Y * CORES
CHUNKS = 8
OUT_ROWS = 128


def coefficient_table():
    theta = math.pi * (np.arange(PTS) + 0.5) / PTS
    cos = lambda m: np.cos(m * theta)[:, None] * np.ones((1, L)) / PTS
    sin = lambda m: np.sin(m * theta)[:, None] * np.ones((1, L)) / PTS
    table = np.zeros((PTS, 16, 2 * L))
    for q in range(4):
        table[:, q, :L] = cos(2 * q + 2)
        table[:, 4 + q, :L] = -sin(2 * q + 2)
        if q < 3:
            table[:, q, L:] = -sin(2 * q + 3)
            table[:, 4 + q, L:] = cos(2 * q + 3)
    for k in range(2 * K):
        table[:, 8 + k, :L] = cos(k + 1)
        table[:, 8 + k, L:] = -sin(k + 1)
    return table.astype(np.float32)


def split(value):
    high = value.astype(jnp.bfloat16)
    low = (value - high.astype(jnp.float32)).astype(jnp.bfloat16)
    return high, low


def dot(first, second):
    return jnp.dot(first, second, preferred_element_type=jnp.float32)


def product(accs, first, second):
    quarter = HANK // 4
    for unit in range(2):
        pltpu.matmul_push_rhs(second[0], 0, unit)
        pltpu.matmul_push_rhs(second[1], 1, unit)
    for unit in range(2):
        for b in range(2):
            part = slice((2 * unit + b) * quarter, (2 * unit + b + 1) * quarter)
            pltpu.matmul_acc_lhs(accs[2 * unit + b], first[0][part], 0 if b == 0 else None)
            pltpu.matmul_acc_lhs(accs[2 * unit + b], first[1][part])
    for unit in range(2):
        for b in range(2):
            part = slice((2 * unit + b) * quarter, (2 * unit + b + 1) * quarter)
            pltpu.matmul_acc_lhs(accs[2 * unit + b], first[0][part], 1 if b == 0 else None)
    return jnp.concatenate([pltpu.matmul_pop(acc) for acc in accs[:4]], axis=0)


def both_products(accs, first, second):
    for unit, (_, right) in enumerate((first, second)):
        pltpu.matmul_push_rhs(right[0], 0, unit)
        pltpu.matmul_push_rhs(right[1], 1, unit)
    half = HANK // 2
    for b in range(2):
        part = slice(b * half, (b + 1) * half)
        for unit, (left, _) in enumerate((first, second)):
            pltpu.matmul_acc_lhs(accs[2 * unit + b], left[0][part], 0 if b == 0 else None)
            pltpu.matmul_acc_lhs(accs[2 * unit + b], left[1][part])
    for b in range(2):
        part = slice(b * half, (b + 1) * half)
        for unit, (left, _) in enumerate((first, second)):
            pltpu.matmul_acc_lhs(accs[2 * unit + b], left[0][part], 1 if b == 0 else None)
    return [jnp.concatenate([pltpu.matmul_pop(accs[2 * u + b]) for b in range(2)], axis=0) for u in range(2)]


def diagonal_sums(full):
    tile = lambda i, h: full[L * i : L * (i + 1), 2 * L * h : 2 * L * (h + 1)]
    return [
        tile(0, 0),
        tile(1, 0),
        tile(2, 0) + tile(0, 1),
        tile(3, 0) + tile(1, 1),
        tile(2, 1),
        tile(3, 1),
    ]


def reduce_body(
    sol, probe, left, sing, right, adj, table, w_out, turned_out,
    solv, probev, factors, singv, tabv, send_a, recv_a, recv_b, recv_c,
    ut_ref, w_ref, zt_ref, u_ref, wt_ref, f_row, f_col, second,
    chunk_sem, small_sem, send_sem, recv_sem, *accs
):
    pts = lax.axis_index("pts")
    rows = lax.axis_index("rows")
    x, core = lax.div(pts, CORES), lax.rem(pts, CORES)
    z, y = lax.div(rows, Y), lax.rem(rows, Y)
    me = y * (X * CORES) + pts
    depth = sol.shape[1]
    size = depth // CHUNKS
    half = depth // 2

    copies = []
    for c in range(CHUNKS):
        if c % (CHUNKS // 2) == 0:
            part = pl.ds((2 * c // CHUNKS) * half, half)
            copy = pltpu.make_async_copy(probe.at[:, part], probev.at[:, part], chunk_sem.at[CHUNKS + 2 * c // CHUNKS])
            copy.start()
            copies.append(copy)
        part = pl.ds(c * size, size)
        copy = pltpu.make_async_copy(sol.at[:, part], solv.at[:, part], chunk_sem.at[c])
        copy.start()
        copies.append(copy)
    tab = pltpu.make_async_copy(table.at[pl.ds(pts * 2, 2)], tabv, small_sem.at[0])
    tab.start()

    owner = (y == 0) | ((y == 1) & (x != 2))
    spots = sorted(
        [(p, j) for p in range(X * CORES) for j in range(Y)],
        key=lambda d: (min(d[0] // CORES, X - d[0] // CORES) + min(d[1], Y - d[1]), -(d[0] % CORES)),
    )
    plane = [(p, z * Y + j, j * (X * CORES) + p) for p, j in spots]
    owners = [
        peer + (j * (X * CORES - p // (3 * CORES) * CORES) + p,)
        for peer, (p, j) in zip(plane, spots)
        if j == 0 or (j == 1 and p // CORES != 2)
    ]
    line = [(pts, lax.rem(z + d, Z) * Y + y, -1) for d in sorted(range(1, Z), key=lambda d: -min(d, Z - d))]
    index = y * (X * CORES - lax.div(x, 3) * CORES) + pts

    def each(peers, action):
        for peer in peers:
            pl.when(me != peer[2])(functools.partial(action, peer))

    barrier = pltpu.get_barrier_semaphore()

    def announce(peer):
        pl.semaphore_signal(barrier, inc=1, device_id=peer[:2], device_id_type=MESH)

    announce((x * CORES + 1 - core, rows))

    @pl.when(owner)
    def _():
        each(plane[::-1], announce)
        for peer in line:
            announce(peer)

    small = [pltpu.make_async_copy(sing, singv, small_sem.at[1])]
    small += [pltpu.make_async_copy(ref, factors.at[i], small_sem.at[2]) for i, ref in enumerate((left, right, adj))]
    for copy in small:
        copy.start()

    tile = 0
    done = iter(copies)
    for c in range(CHUNKS):
        if c % (CHUNKS // 2) == 0:
            next(done).wait()
        next(done).wait()
        for start in range(c * size, (c + 1) * size, HANK):
            part = pl.ds(start, HANK)
            unit, register = tile % 2, tile // 2 % 2
            pltpu.matmul_push_rhs(jnp.concatenate([solv[0, part, :], solv[1, part, :]], axis=1), register, unit)
            pltpu.matmul_acc_lhs(accs[2 * unit], probev[:, part], register)
            tile += 1
    gram = pltpu.matmul_pop(accs[0]) + pltpu.matmul_pop(accs[2])
    tab.wait()
    for q in range(4):
        total = None
        for p in range(2):
            own = gram[:, 128 * p : 128 * (p + 1)]
            term = own * tabv[p, q : q + 1, :] + pltpu.roll(own, L, 1) * tabv[p, 4 + q : 5 + q, :]
            total = term if total is None else total + term
        if q < 3:
            send_a[L * q : L * (q + 1), :] = total
        else:
            send_a[L * q :, :] = total[: L // 2] + pltpu.roll(total[L // 2 :], L, 1)

    def piece(index):
        return pl.ds(pl.multiple_of(index * PIECE, PIECE), PIECE)

    def send(source, target, phase, peer):
        pltpu.make_async_remote_copy(
            src_ref=source(peer),
            dst_ref=target,
            send_sem=send_sem.at[0],
            recv_sem=recv_sem.at[phase],
            device_id=peer[:2],
            device_id_type=MESH,
        ).start()

    def arrived(ref, count, phase):
        ref = ref.at[pl.ds(0, count * PIECE)]
        pltpu.make_async_copy(ref, ref, recv_sem.at[phase]).wait()

    mine, here = piece(index), piece(z)

    @pl.when(owner)
    def _():
        pl.semaphore_wait(barrier, OWNERS + Z - 1)

    @pl.when(jnp.logical_not(owner))
    def _():
        pl.semaphore_wait(barrier, OWNERS + 1)

    each(owners[::-1], functools.partial(send, lambda peer: send_a.at[piece(peer[3])], recv_a.at[piece(me)], 0))

    def keep(ref, value):
        ref[0], ref[1] = split(value)

    def turn(first, last):
        step = half // 8
        for t in range(first, last):
            pair = [probev[:, h * half + t * step : h * half + (t + 1) * step] for h in range(2)]
            turned_out[t * step : (t + 1) * step, :] = jnp.concatenate(pair, axis=0).T

    @pl.when(owner)
    def _():
        recv_a[piece(me), :] = send_a[mine, :]

    small[0].wait()
    pltpu.make_async_copy(factors, factors, small_sem.at[2]).wait()
    s_row = jnp.broadcast_to(singv[...], (HANK, HANK))
    zbar = factors[2] / s_row
    keep(ut_ref, factors[0].T)
    keep(u_ref, factors[0])
    keep(w_ref, factors[1])
    keep(wt_ref, factors[1].T)
    keep(zt_ref, zbar.T)
    turn(0, 4)

    @pl.when(owner)
    def _():
        arrived(recv_a, GROUP - 1, 0)
        recv_b[here, :] = jnp.sum(recv_a[...].reshape(GROUP, PIECE, 128), axis=0)
        for peer in line:
            send(lambda peer: recv_b.at[here], recv_b.at[here], 1, peer)

    row_id = lax.broadcasted_iota(jnp.int32, (HANK, HANK), 0)
    col_id = lax.broadcasted_iota(jnp.int32, (HANK, HANK), 1)
    eye = row_id == col_id
    s_col = s_row.T
    recip = jnp.where(eye, 0.0, 1.0 / jnp.where(eye, 1.0, s_row * s_row - s_col * s_col))
    f_row[...] = recip * s_row
    f_col[...] = recip * s_col
    second_bar = product(accs, split(product(accs, u_ref, split(zbar))), wt_ref)
    for m, value in enumerate(diagonal_sums(second_bar)):
        second[m] = value

    @pl.when(owner)
    def _():
        arrived(recv_b, Z - 1, 1)
        recv_c[mine, :] = jnp.sum(recv_b[...].reshape(Z, PIECE, 128), axis=0)
        each(plane, functools.partial(send, lambda peer: recv_c.at[mine], recv_c.at[mine], 2))

    turn(4, 8)

    @pl.when(owner)
    def _():
        arrived(recv_c, OWNERS - 1, 2)

    @pl.when(jnp.logical_not(owner))
    def _():
        arrived(recv_c, OWNERS, 2)

    lane = lax.broadcasted_iota(jnp.int32, (L, 2 * L), 1)
    low = lane < L
    even = [recv_c[L * q : L * (q + 1), :] for q in range(3)]
    last = recv_c[3 * L :, :]
    turned = [pltpu.roll(value, L, 1) for value in even]
    turned.append(jnp.concatenate([pltpu.roll(last, L, 1), last], axis=0))
    pairs = []
    for q in range(3):
        pairs.append(even[q])
        pairs.append(jnp.where(low, turned[q], turned[q + 1]))
    hankel = jnp.concatenate(
        [jnp.concatenate([pairs[i], pairs[i + 2]], axis=1) for i in range(K)], axis=0
    )
    quot = product(accs, ut_ref, split(hankel))
    zmat = product(accs, split(quot), w_ref)
    parts = split(zmat)
    left_term, right_term = both_products(accs[4:], (parts, zt_ref), (zt_ref, parts))
    sing_row = singv[...]
    sbar = -jnp.sum(factors[2] * zmat, axis=0, keepdims=True) / (sing_row * sing_row)
    core_mat = (
        f_row[...] * (left_term - left_term.T)
        - f_col[...] * (right_term - right_term.T)
        + jnp.where(eye, jnp.broadcast_to(sbar, (HANK, HANK)), 0.0)
    )
    first_bar = product(accs, split(product(accs, u_ref, split(core_mat))), wt_ref)

    sums = diagonal_sums(first_bar)
    sums = [sums[0]] + [sums[m] + second[m - 1] for m in range(1, 6)] + [second[5]]
    weights = [jnp.zeros((L, 2 * L), jnp.float32) for p in range(2)]
    zero = jnp.zeros((L, 2 * L), jnp.float32)
    for k in range(2 * K):
        here_k = sums[k] if k < 7 else zero
        before = sums[k - 1] if k > 0 else zero
        mixed = jnp.where(low, here_k, before)
        both = mixed + pltpu.roll(mixed, L, 1)
        for p in range(2):
            weights[p] = weights[p] + both * tabv[p, 8 + k : 9 + k, :]
    for p in range(2):
        w_out[:, 128 * p : 128 * (p + 1)] = weights[p].astype(jnp.bfloat16)

    def all_sent(count):
        sent = solv.at[0, pl.ds(0, 2 * PIECE * count)]
        pltpu.make_async_copy(sent, sent, send_sem.at[0]).wait()

    @pl.when(owner)
    def _():
        all_sent(OWNERS - 1 + Z - 1 + GROUP - 1)

    @pl.when(jnp.logical_not(owner))
    def _():
        all_sent(OWNERS)


def reduce_kernel(*refs):
    parts = [
        pltpu.ACC(unit)((HANK // share, HANK), jnp.float32) for share in (4, 2) for unit in (0, 0, 1, 1)
    ]
    pl.run_scoped(functools.partial(reduce_body, *refs), *parts)


def output_kernel(turned, w_ref, out, held, sem):
    half = turned.shape[0]
    size = OUT_ROWS
    zero = jnp.zeros((L, 256), jnp.bfloat16)
    wide = [jnp.concatenate([w_ref[...], zero], axis=0), jnp.concatenate([zero, w_ref[...]], axis=0)]
    for c in range(half // size):
        block = turned[c * size : (c + 1) * size, :]
        for h in range(2):
            res = dot(block, wide[h]).astype(jnp.bfloat16)
            part = pl.ds(h * half + c * size, size)
            for p in range(2):
                held[p, part, :] = res[:, 128 * p : 128 * (p + 1)]
            pltpu.make_async_copy(held.at[:, part], out.at[:, part], sem.at[0]).start()
    pltpu.make_async_copy(held, out, sem.at[0]).wait()


def per_device(solutions, probe, left_factor, singular, right_factor, reduced_adjoint):
    table = jnp.asarray(coefficient_table())
    depth = solutions.shape[1]
    hbm = pl.BlockSpec(memory_space=pltpu.HBM)
    vmem = pl.BlockSpec(memory_space=pltpu.VMEM)
    f32 = lambda *shape: pltpu.VMEM(shape, jnp.float32)
    bf16 = lambda *shape: pltpu.VMEM(shape, jnp.bfloat16)
    weights, turned = pl.pallas_call(
        reduce_kernel,
        name="moments",
        out_shape=[
            jax.ShapeDtypeStruct((L, 256), jnp.bfloat16),
            jax.ShapeDtypeStruct((depth // 2, 128), jnp.bfloat16),
        ],
        in_specs=[hbm] * 7,
        out_specs=[vmem] * 2,
        scratch_shapes=[
            bf16(2, depth, 128), bf16(L, depth), f32(3, HANK, HANK), f32(1, HANK), f32(2, 16, 128),
            f32(OWNERS * PIECE, 128), f32(GROUP * PIECE, 128), f32(Z * PIECE, 128), f32(OWNERS * PIECE, 128),
            *[bf16(2, HANK, HANK)] * 5, f32(HANK, HANK), f32(HANK, HANK), f32(6, L, 2 * L),
            pltpu.SemaphoreType.DMA((CHUNKS + 2,)), pltpu.SemaphoreType.DMA((3,)),
            pltpu.SemaphoreType.DMA((1,)), pltpu.SemaphoreType.DMA((3,)),
        ],
        compiler_params=pltpu.CompilerParams(
            collective_id=0, has_side_effects=True, vmem_limit_bytes=24 << 20
        ),
    )(
        *(
            pltpu.with_memory_space_constraint(array, pltpu.HBM)
            for array in (
                solutions, probe, left_factor, singular.reshape(1, HANK), right_factor, reduced_adjoint, table
            )
        )
    )
    return pl.pallas_call(
        output_kernel,
        name="output",
        out_shape=jax.ShapeDtypeStruct((2, depth, 128), jnp.bfloat16),
        in_specs=[vmem] * 2,
        out_specs=pl.BlockSpec(memory_space=pltpu.HBM),
        scratch_shapes=[bf16(2, depth, 128), pltpu.SemaphoreType.DMA((1,))],
        compiler_params=pltpu.CompilerParams(vmem_limit_bytes=24 << 20),
    )(turned, weights)


def solution(mesh):
    in_specs = (P("pts", "rows", None), P(None, "rows"), P(), P(), P(), P())
    out_specs = P("pts", "rows", None)
    return jax.shard_map(
        per_device, mesh=mesh, in_specs=in_specs, out_specs=out_specs, check_vma=False
    )
```

```python
import functools
import math

import jax
import jax.numpy as jnp
import numpy as np
from jax import lax
from jax.experimental import pallas as pl
from jax.experimental.pallas import tpu as pltpu
from jax.sharding import PartitionSpec as P

L = 64
K = 4
HANK = 256
PTS = 16
MESH = pl.DeviceIdType.MESH
X, Y, Z, CORES = 4, 4, 8, 2
OWNERS = 14
PIECE = 16
GROUP = X * Y * CORES
CHUNKS = 8
OUT_ROWS = 128


def coefficient_table():
    theta = math.pi * (np.arange(PTS) + 0.5) / PTS
    cos = lambda m: np.cos(m * theta)[:, None] * np.ones((1, L)) / PTS
    sin = lambda m: np.sin(m * theta)[:, None] * np.ones((1, L)) / PTS
    table = np.zeros((PTS, 16, 2 * L))
    for q in range(4):
        table[:, q, :L] = cos(2 * q + 2)
        table[:, 4 + q, :L] = -sin(2 * q + 2)
        if q < 3:
            table[:, q, L:] = -sin(2 * q + 3)
            table[:, 4 + q, L:] = cos(2 * q + 3)
    for k in range(2 * K):
        table[:, 8 + k, :L] = cos(k + 1)
        table[:, 8 + k, L:] = -sin(k + 1)
    return table.astype(np.float32)


def split(value):
    high = value.astype(jnp.bfloat16)
    low = (value - high.astype(jnp.float32)).astype(jnp.bfloat16)
    return high, low


def dot(first, second):
    return jnp.dot(first, second, preferred_element_type=jnp.float32)


def product(accs, first, second):
    quarter = HANK // 4
    for unit in range(2):
        pltpu.matmul_push_rhs(second[0], 0, unit)
        pltpu.matmul_push_rhs(second[1], 1, unit)
    for unit in range(2):
        for b in range(2):
            part = slice((2 * unit + b) * quarter, (2 * unit + b + 1) * quarter)
            pltpu.matmul_acc_lhs(accs[2 * unit + b], first[0][part], 0 if b == 0 else None)
            pltpu.matmul_acc_lhs(accs[2 * unit + b], first[1][part])
    for unit in range(2):
        for b in range(2):
            part = slice((2 * unit + b) * quarter, (2 * unit + b + 1) * quarter)
            pltpu.matmul_acc_lhs(accs[2 * unit + b], first[0][part], 1 if b == 0 else None)
    return jnp.concatenate([pltpu.matmul_pop(acc) for acc in accs[:4]], axis=0)


def both_products(accs, first, second):
    for unit, (_, right) in enumerate((first, second)):
        pltpu.matmul_push_rhs(right[0], 0, unit)
        pltpu.matmul_push_rhs(right[1], 1, unit)
    half = HANK // 2
    for b in range(2):
        part = slice(b * half, (b + 1) * half)
        for unit, (left, _) in enumerate((first, second)):
            pltpu.matmul_acc_lhs(accs[2 * unit + b], left[0][part], 0 if b == 0 else None)
            pltpu.matmul_acc_lhs(accs[2 * unit + b], left[1][part])
    for b in range(2):
        part = slice(b * half, (b + 1) * half)
        for unit, (left, _) in enumerate((first, second)):
            pltpu.matmul_acc_lhs(accs[2 * unit + b], left[0][part], 1 if b == 0 else None)
    return [jnp.concatenate([pltpu.matmul_pop(accs[2 * u + b]) for b in range(2)], axis=0) for u in range(2)]


def diagonal_sums(full):
    tile = lambda i, h: full[L * i : L * (i + 1), 2 * L * h : 2 * L * (h + 1)]
    return [
        tile(0, 0),
        tile(1, 0),
        tile(2, 0) + tile(0, 1),
        tile(3, 0) + tile(1, 1),
        tile(2, 1),
        tile(3, 1),
    ]


def reduce_body(
    sol, probe, left, sing, right, adj, table, w_out, turned_out,
    solv, probev, factors, singv, tabv, send_a, recv_a, recv_b, recv_c,
    ut_ref, w_ref, zt_ref, u_ref, wt_ref, f_row, f_col, second,
    chunk_sem, small_sem, send_sem, recv_sem, *accs
):
    pts = lax.axis_index("pts")
    rows = lax.axis_index("rows")
    x, core = lax.div(pts, CORES), lax.rem(pts, CORES)
    z, y = lax.div(rows, Y), lax.rem(rows, Y)
    me = y * (X * CORES) + pts
    depth = sol.shape[1]
    size = depth // CHUNKS
    half = depth // 2

    copies = []
    for c in range(CHUNKS):
        if c % (CHUNKS // 2) == 0:
            part = pl.ds((2 * c // CHUNKS) * half, half)
            copy = pltpu.make_async_copy(probe.at[:, part], probev.at[:, part], chunk_sem.at[CHUNKS + 2 * c // CHUNKS])
            copy.start()
            copies.append(copy)
        part = pl.ds(c * size, size)
        copy = pltpu.make_async_copy(sol.at[:, part], solv.at[:, part], chunk_sem.at[c])
        copy.start()
        copies.append(copy)
    tab = pltpu.make_async_copy(table.at[pl.ds(pts * 2, 2)], tabv, small_sem.at[0])
    tab.start()

    owner = (y == 0) | ((y == 1) & (x != 2))
    spots = sorted(
        [(p, j) for p in range(X * CORES) for j in range(Y)],
        key=lambda d: (min(d[0] // CORES, X - d[0] // CORES) + min(d[1], Y - d[1]), -(d[0] % CORES)),
    )
    plane = [(p, z * Y + j, j * (X * CORES) + p) for p, j in spots]
    owners = [
        peer + (j * (X * CORES - p // (3 * CORES) * CORES) + p,)
        for peer, (p, j) in zip(plane, spots)
        if j == 0 or (j == 1 and p // CORES != 2)
    ]
    line = [(pts, lax.rem(z + d, Z) * Y + y, -1) for d in sorted(range(1, Z), key=lambda d: -min(d, Z - d))]
    index = lax.rem(y * (X * CORES - lax.div(x, 3) * CORES) + pts, OWNERS)

    def each(peers, action):
        for peer in peers:
            pl.when(me != peer[2])(functools.partial(action, peer))

    barrier = pltpu.get_barrier_semaphore()

    def announce(peer):
        pl.semaphore_signal(barrier, inc=1, device_id=peer[:2], device_id_type=MESH)

    announce((x * CORES + 1 - core, rows))

    @pl.when(owner)
    def _():
        each(plane[::-1], announce)
        for peer in line:
            announce(peer)

    small = [pltpu.make_async_copy(sing, singv, small_sem.at[1])]
    small += [pltpu.make_async_copy(ref, factors.at[i], small_sem.at[2]) for i, ref in enumerate((left, right, adj))]
    for copy in small:
        copy.start()

    tile = 0
    done = iter(copies)
    for c in range(CHUNKS):
        if c % (CHUNKS // 2) == 0:
            next(done).wait()
        next(done).wait()
        for start in range(c * size, (c + 1) * size, HANK):
            part = pl.ds(start, HANK)
            unit, register = tile % 2, tile // 2 % 2
            pltpu.matmul_push_rhs(jnp.concatenate([solv[0, part, :], solv[1, part, :]], axis=1), register, unit)
            pltpu.matmul_acc_lhs(accs[2 * unit], probev[:, part], register)
            tile += 1
    gram = pltpu.matmul_pop(accs[0]) + pltpu.matmul_pop(accs[2])
    tab.wait()
    for q in range(4):
        total = None
        for p in range(2):
            own = gram[:, 128 * p : 128 * (p + 1)]
            term = own * tabv[p, q : q + 1, :] + pltpu.roll(own, L, 1) * tabv[p, 4 + q : 5 + q, :]
            total = term if total is None else total + term
        if q < 3:
            send_a[L * q : L * (q + 1), :] = total
        else:
            send_a[L * q :, :] = total[: L // 2] + pltpu.roll(total[L // 2 :], L, 1)

    def piece(index):
        return pl.ds(pl.multiple_of(index * PIECE, PIECE), PIECE)

    def send(source, target, phase, peer):
        pltpu.make_async_remote_copy(
            src_ref=source(peer),
            dst_ref=target,
            send_sem=send_sem.at[0],
            recv_sem=recv_sem.at[phase],
            device_id=peer[:2],
            device_id_type=MESH,
        ).start()

    def arrived(ref, count, phase):
        ref = ref.at[pl.ds(0, count * PIECE)]
        pltpu.make_async_copy(ref, ref, recv_sem.at[phase]).wait()

    mine, here = piece(index), piece(z)

    @pl.when(owner)
    def _():
        pl.semaphore_wait(barrier, OWNERS + Z - 1)

    @pl.when(jnp.logical_not(owner))
    def _():
        pl.semaphore_wait(barrier, OWNERS + 1)

    each(owners[::-1], functools.partial(send, lambda peer: send_a.at[piece(peer[3])], recv_a.at[piece(me)], 0))

    def keep(ref, value):
        ref[0], ref[1] = split(value)

    def turn(first, last):
        step = half // 8
        for t in range(first, last):
            pair = [probev[:, h * half + t * step : h * half + (t + 1) * step] for h in range(2)]
            turned_out[t * step : (t + 1) * step, :] = jnp.concatenate(pair, axis=0).T

    @pl.when(owner)
    def _():
        recv_a[piece(me), :] = send_a[mine, :]

    small[0].wait()
    pltpu.make_async_copy(factors, factors, small_sem.at[2]).wait()
    s_row = jnp.broadcast_to(singv[...], (HANK, HANK))
    zbar = factors[2] / s_row
    keep(ut_ref, factors[0].T)
    keep(u_ref, factors[0])
    keep(w_ref, factors[1])
    keep(wt_ref, factors[1].T)
    keep(zt_ref, zbar.T)
    turn(0, 4)

    @pl.when(owner)
    def _():
        arrived(recv_a, GROUP - 1, 0)
        recv_b[here, :] = jnp.sum(recv_a[...].reshape(GROUP, PIECE, 128), axis=0)
        for peer in line:
            send(lambda peer: recv_b.at[here], recv_b.at[here], 1, peer)

    row_id = lax.broadcasted_iota(jnp.int32, (HANK, HANK), 0)
    col_id = lax.broadcasted_iota(jnp.int32, (HANK, HANK), 1)
    eye = row_id == col_id
    s_col = s_row.T
    recip = jnp.where(eye, 0.0, 1.0 / jnp.where(eye, 1.0, s_row * s_row - s_col * s_col))
    f_row[...] = recip * s_row
    f_col[...] = recip * s_col
    second_bar = product(accs, split(product(accs, u_ref, split(zbar))), wt_ref)
    for m, value in enumerate(diagonal_sums(second_bar)):
        second[m] = value

    @pl.when(owner)
    def _():
        arrived(recv_b, Z - 1, 1)
        recv_c[mine, :] = jnp.sum(recv_b[...].reshape(Z, PIECE, 128), axis=0)
        each(plane, functools.partial(send, lambda peer: recv_c.at[mine], recv_c.at[mine], 2))

    turn(4, 8)

    @pl.when(owner)
    def _():
        arrived(recv_c, OWNERS - 1, 2)

    @pl.when(jnp.logical_not(owner))
    def _():
        arrived(recv_c, OWNERS, 2)

    lane = lax.broadcasted_iota(jnp.int32, (L, 2 * L), 1)
    low = lane < L
    even = [recv_c[L * q : L * (q + 1), :] for q in range(3)]
    last = recv_c[3 * L :, :]
    turned = [pltpu.roll(value, L, 1) for value in even]
    turned.append(jnp.concatenate([pltpu.roll(last, L, 1), last], axis=0))
    pairs = []
    for q in range(3):
        pairs.append(even[q])
        pairs.append(jnp.where(low, turned[q], turned[q + 1]))
    hankel = jnp.concatenate(
        [jnp.concatenate([pairs[i], pairs[i + 2]], axis=1) for i in range(K)], axis=0
    )
    quot = product(accs, ut_ref, split(hankel))
    zmat = product(accs, split(quot), w_ref)
    parts = split(zmat)
    left_term, right_term = both_products(accs[4:], (parts, zt_ref), (zt_ref, parts))
    sing_row = singv[...]
    sbar = -jnp.sum(factors[2] * zmat, axis=0, keepdims=True) / (sing_row * sing_row)
    core_mat = (
        f_row[...] * (left_term - left_term.T)
        - f_col[...] * (right_term - right_term.T)
        + jnp.where(eye, jnp.broadcast_to(sbar, (HANK, HANK)), 0.0)
    )
    first_bar = product(accs, split(product(accs, u_ref, split(core_mat))), wt_ref)

    sums = diagonal_sums(first_bar)
    sums = [sums[0]] + [sums[m] + second[m - 1] for m in range(1, 6)] + [second[5]]
    weights = [jnp.zeros((L, 2 * L), jnp.float32) for p in range(2)]
    zero = jnp.zeros((L, 2 * L), jnp.float32)
    for k in range(2 * K):
        here_k = sums[k] if k < 7 else zero
        before = sums[k - 1] if k > 0 else zero
        mixed = jnp.where(low, here_k, before)
        both = mixed + pltpu.roll(mixed, L, 1)
        for p in range(2):
            weights[p] = weights[p] + both * tabv[p, 8 + k : 9 + k, :]
    for p in range(2):
        w_out[:, 128 * p : 128 * (p + 1)] = weights[p].astype(jnp.bfloat16)

    def all_sent(count):
        sent = solv.at[0, pl.ds(0, 2 * PIECE * count)]
        pltpu.make_async_copy(sent, sent, send_sem.at[0]).wait()

    @pl.when(owner)
    def _():
        all_sent(OWNERS - 1 + Z - 1 + GROUP - 1)

    @pl.when(jnp.logical_not(owner))
    def _():
        all_sent(OWNERS)


def reduce_kernel(*refs):
    parts = [
        pltpu.ACC(unit)((HANK // share, HANK), jnp.float32) for share in (4, 2) for unit in (0, 0, 1, 1)
    ]
    pl.run_scoped(functools.partial(reduce_body, *refs), *parts)


def output_kernel(turned, w_ref, out, held, sem):
    half = turned.shape[0]
    size = OUT_ROWS
    zero = jnp.zeros((L, 256), jnp.bfloat16)
    wide = [jnp.concatenate([w_ref[...], zero], axis=0), jnp.concatenate([zero, w_ref[...]], axis=0)]
    for c in range(half // size):
        block = turned[c * size : (c + 1) * size, :]
        for h in range(2):
            res = dot(block, wide[h]).astype(jnp.bfloat16)
            part = pl.ds(h * half + c * size, size)
            for p in range(2):
                held[p, part, :] = res[:, 128 * p : 128 * (p + 1)]
            pltpu.make_async_copy(held.at[:, part], out.at[:, part], sem.at[0]).start()
    pltpu.make_async_copy(held, out, sem.at[0]).wait()


def per_device(solutions, probe, left_factor, singular, right_factor, reduced_adjoint):
    table = jnp.asarray(coefficient_table())
    depth = solutions.shape[1]
    hbm = pl.BlockSpec(memory_space=pltpu.HBM)
    vmem = pl.BlockSpec(memory_space=pltpu.VMEM)
    f32 = lambda *shape: pltpu.VMEM(shape, jnp.float32)
    bf16 = lambda *shape: pltpu.VMEM(shape, jnp.bfloat16)
    weights, turned = pl.pallas_call(
        reduce_kernel,
        name="moments",
        out_shape=[
            jax.ShapeDtypeStruct((L, 256), jnp.bfloat16),
            jax.ShapeDtypeStruct((depth // 2, 128), jnp.bfloat16),
        ],
        in_specs=[hbm] * 7,
        out_specs=[vmem] * 2,
        scratch_shapes=[
            bf16(2, depth, 128), bf16(L, depth), f32(3, HANK, HANK), f32(1, HANK), f32(2, 16, 128),
            f32(OWNERS * PIECE, 128), f32(GROUP * PIECE, 128), f32(Z * PIECE, 128), f32(OWNERS * PIECE, 128),
            *[bf16(2, HANK, HANK)] * 5, f32(HANK, HANK), f32(HANK, HANK), f32(6, L, 2 * L),
            pltpu.SemaphoreType.DMA((CHUNKS + 2,)), pltpu.SemaphoreType.DMA((3,)),
            pltpu.SemaphoreType.DMA((1,)), pltpu.SemaphoreType.DMA((3,)),
        ],
        compiler_params=pltpu.CompilerParams(
            collective_id=0, has_side_effects=True, vmem_limit_bytes=24 << 20
        ),
    )(
        *(
            pltpu.with_memory_space_constraint(array, pltpu.HBM)
            for array in (
                solutions, probe, left_factor, singular.reshape(1, HANK), right_factor, reduced_adjoint, table
            )
        )
    )
    return pl.pallas_call(
        output_kernel,
        name="output",
        out_shape=jax.ShapeDtypeStruct((2, depth, 128), jnp.bfloat16),
        in_specs=[vmem] * 2,
        out_specs=pl.BlockSpec(memory_space=pltpu.HBM),
        scratch_shapes=[bf16(2, depth, 128), pltpu.SemaphoreType.DMA((1,))],
        compiler_params=pltpu.CompilerParams(vmem_limit_bytes=24 << 20),
    )(turned, weights)


def solution(mesh):
    in_specs = (P("pts", "rows", None), P(None, "rows"), P(), P(), P(), P())
    out_specs = P("pts", "rows", None)
    return jax.shard_map(
        per_device, mesh=mesh, in_specs=in_specs, out_specs=out_specs, check_vma=False
    )
```
